256 devices in a mesh: dom: 128 (over x, y, z), feat: 2 (over core).
Axes of the slice: x: 4, y: 4, z: 8, core: 2. Of those that a mesh axis runs over, the one named last changes fastest.
Arguments:
- history: bfloat16 [131072, 256], P('dom', 'feat'), may hold values from -6 to 6
- pull_list: int32 [128, 128, 2], P('dom'), may hold values from -1 to 7, as said below
- remote_tiles: bfloat16 [128, 128, 2, 128, 128], P('dom'), may hold values from -0.1875 to 0.1875
- remote_dst: int32 [128, 128, 2], P('dom'), may hold values from 0 to 15
- local_tiles: bfloat16 [8192, 128, 128], P('dom'), may hold values from -0.1875 to 0.1875
- local_src: int32 [128, 64], P('dom'), may hold values from 0 to 7
- local_dst: int32 [128, 64], P('dom'), may hold values from 0 to 15
- weight: bfloat16 [256, 256], P(None, 'feat'), may hold values from -0.375 to 0.375
- bias: float32 [256], P('feat'), may hold values from -3 to 3
- cotangent: bfloat16 [131072, 256], P('dom', 'feat'), may hold values from -0.015625 to 0.015625
Outputs:
- new_rows: bfloat16 [131072, 256], P('dom', 'feat')
- grad_weight: float32 [256, 256], P(None, 'feat')
- grad_bias: float32 [256], P('feat')
The draws below stay inside these ranges and needn't reach their ends.
Inputs may be any that keep to these rules, and one draw needn't show every extreme that they name: pull_list[r, o, c] is -1 or a block index local to owner o; in each (r, o) the used entries come first and are distinct; pull_list[r, r] is all -1; every other (r, o) asks 2 or 1 blocks; every partition asks 2 blocks of the next partition, and some owner is asked for 2 blocks by every other partition.
All inputs are finite; a program needn't handle non-finite values.
Results may differ from the reference program's by a relative error of at most 0.0065.
Values may be sent and summed in bfloat16 or wider, within the bound.
A program may use at most 128 MiB of HBM per device.

```python
import jax
import jax.numpy as jnp
from jax import lax

F = 256
BLK = 128
CAP = 2
NB = 8
NL = 64
NODES = 131072
LTILES = 8192
N_DOM = 128


def draw_pull_list(key, part):
    key_a, key_c, key_d = jax.random.split(key, 3)
    dropped = jax.random.randint(key_a, (N_DOM, N_DOM), 0, 16) == 0
    counts = jnp.where(dropped, CAP - 1, CAP)
    requester = jnp.arange(N_DOM, dtype=jnp.int32)[:, None]
    owner = jnp.arange(N_DOM, dtype=jnp.int32)[None, :]
    full_owner = jax.random.randint(key_c, (), 0, N_DOM)
    counts = jnp.where(owner == full_owner, CAP, counts)
    counts = jnp.where(owner == (requester + 1) % N_DOM, CAP, counts)
    counts = jnp.where(owner == requester, 0, counts)
    offset = jax.random.randint(key_d, (N_DOM, N_DOM), 0, NB)
    slot_ids = jnp.arange(CAP, dtype=jnp.int32)
    chosen = (offset[:, :, None] + slot_ids[None, None, :]) % NB
    return jnp.where(slot_ids[None, None, :] < counts[:, :, None], chosen, -1).astype(jnp.int32)


def with_ends(drawn, key, low, high):
    extent = drawn.shape
    spot = [jax.random.randint(jax.random.fold_in(key, axis), (), 0, extent[axis]) for axis in range(len(extent))]
    drawn = drawn.at[tuple(spot)].set(low)
    longest = extent.index(max(extent))
    spot[longest] = (spot[longest] + 1) % extent[longest]
    return drawn.at[tuple(spot)].set(high)


def shard_levels(key, extent, pieces, low, top_value):
    loudness = 1.0
    for axis_at, blocks in pieces:
        draws = jax.random.uniform(jax.random.fold_in(jax.random.fold_in(key, 6), axis_at), (blocks,), jnp.float32, low / len(pieces), top_value / len(pieces))
        loudness = loudness * jnp.repeat(jnp.exp(draws), extent[axis_at] // blocks).reshape((-1,) + (1,) * (len(extent) - 1 - axis_at))
    return loudness


def centred(own_key, shape, spread, reach, pieces=(), held_as=jnp.bfloat16):
    array = jax.random.normal(own_key, shape, jnp.float32) * spread
    if len(pieces) > 0:
        array = shard_levels(own_key, shape, pieces, -0.22, 0.18) * array
    return jnp.clip(array, min=-reach, max=reach).astype(held_as)


def setup_inputs(seed: int = 0) -> dict:
    streams_of = jax.random.split(jax.random.key(seed), 11)
    history = centred(streams_of[0], (NODES, F), 1.0, 6.0, ((0, 128), (1, 2)))
    pull_list = draw_pull_list(jax.random.fold_in(streams_of[10], 71), 0)
    remote_tiles = centred(streams_of[2], (N_DOM, N_DOM, CAP, BLK, BLK), (8 * BLK) ** -0.5, 0.1875, ((0, 128),))
    remote_dst = with_ends(jax.random.randint(streams_of[3], (N_DOM, N_DOM, CAP), 0, 2 * NB), jax.random.fold_in(streams_of[3], 1), 0, (2 * NB) - 1).astype(jnp.int32)
    local_tiles = centred(streams_of[4], (LTILES, BLK, BLK), (8 * BLK) ** -0.5, 0.1875, ((0, 128),))
    local_src = with_ends(jax.random.randint(streams_of[5], (N_DOM, NL), 0, NB), jax.random.fold_in(streams_of[5], 1), 0, NB - 1).astype(jnp.int32)
    local_dst = with_ends(jax.random.randint(streams_of[6], (N_DOM, NL), 0, 2 * NB), jax.random.fold_in(streams_of[6], 1), 0, (2 * NB) - 1).astype(jnp.int32)
    weight = centred(streams_of[7], (F, F), F ** -0.5, 0.375, ((1, 2),))
    bias = centred(streams_of[8], (F,), 0.5, 3.0, ((0, 2),), jnp.float32)
    cotangent = centred(streams_of[9], (NODES, F), NODES ** -0.5, 0.015625, ((0, 128), (1, 2)))
    return {"history": history, "pull_list": pull_list, "remote_tiles": remote_tiles, "remote_dst": remote_dst, "local_tiles": local_tiles, "local_src": local_src, "local_dst": local_dst, "weight": weight, "bias": bias, "cotangent": cotangent}


def activate(value):
    return jax.nn.gelu(value, approximate=True)

def reference(history, pull_list, remote_tiles, remote_dst, local_tiles, local_src, local_dst, weight, bias, cotangent):
    blocks = history.reshape(N_DOM * NB, BLK, F)
    local_set = local_tiles.reshape(N_DOM, NL, BLK, BLK)
    row_ids = jnp.arange(2 * NB, dtype=jnp.int32)[:, None]

    def per_device(device):
        wanted = pull_list[device]
        owner_ids = jnp.arange(N_DOM, dtype=jnp.int32)[:, None]
        block_ids = (owner_ids * NB + jnp.clip(wanted, 0, NB - 1)).astype(jnp.int32)
        pulled = jnp.where((wanted >= 0)[:, :, None, None], blocks[block_ids], jnp.zeros((), blocks.dtype))
        products = jnp.einsum('ockj,ocjf->ockf', remote_tiles[device].astype(jnp.float32), pulled.astype(jnp.float32))
        pick_remote = (remote_dst[device].reshape(-1)[None, :] == row_ids).astype(jnp.float32)
        partial_value = jnp.dot(pick_remote, products.reshape(N_DOM * CAP, BLK * F), precision=lax.Precision.HIGHEST)
        sources = blocks[(device * NB + local_src[device]).astype(jnp.int32)]
        local_prod = jnp.einsum('kij,kjf->kif', local_set[device].astype(jnp.float32), sources.astype(jnp.float32))
        pick_local = (local_dst[device][None, :] == row_ids).astype(jnp.float32)
        return partial_value + jnp.dot(pick_local, local_prod.reshape(NL, BLK * F), precision=lax.Precision.HIGHEST)
    partials = lax.map(per_device, jnp.arange(N_DOM, dtype=jnp.int32))
    aggregate = partials[:, :NB] + jnp.roll(partials[:, NB:], 1, axis=0)
    aggregate = aggregate.reshape(NODES, F).astype(jnp.bfloat16)
    preact = jnp.dot(aggregate, weight, preferred_element_type=jnp.float32) + bias
    new_rows, backward_fn = jax.vjp(activate, preact)
    grad_pre = backward_fn(cotangent.astype(jnp.float32))[0].astype(jnp.bfloat16)
    grad_weight = lax.dot_general(aggregate, grad_pre, (((0,), (0,)), ((), ())), preferred_element_type=jnp.float32)
    grad_bias = lax.optimization_barrier(jnp.sum(grad_pre.astype(jnp.float32), axis=0))
    return (new_rows.astype(jnp.bfloat16), grad_weight, grad_bias)
```

```python
import functools

import jax
import jax.numpy as jnp
from jax import lax
from jax.sharding import PartitionSpec as P
from jax.experimental import pallas as pl
from jax.experimental.pallas import tpu as pltpu

MESH = pl.DeviceIdType.MESH
X, Y, Z = 0, 1, 2
SIZES = (4, 4, 8)
STRIDES = (32, 8, 1)
NB = 8
BLK = 128
HALF = 128
SLICE = 32
KINDS = ((Z, Y, X), (Z, X, Y), (Y, Z, X), (X, Z, Y))


def coords():
    p = lax.axis_index("dom")
    return (p // 32, lax.rem(p // 8, 4), lax.rem(p, 8)), lax.axis_index("feat")


def moved(me, axis, offset):
    n = SIZES[axis]
    there = list(me)
    there[axis] = lax.rem(me[axis] + (offset % n), n)
    return there[0] * 32 + there[1] * 8 + there[2]


def pull_kernel(hist, plist, pulled, *scratch):
    sets = [scratch[0:4], scratch[4:8], scratch[8:16], scratch[16:24]]
    packs = scratch[24:28]
    lists_v, lists_s, send_sems, recv_sems, local_sems = scratch[28:33]
    me, f = coords()
    used = [0, 0]
    remote_copies = []
    local_copies = []

    def remote(src, dst, axis, offset):
        i = used[0]
        used[0] += 1
        copy = pltpu.make_async_remote_copy(
            src_ref=src,
            dst_ref=dst,
            send_sem=send_sems.at[i],
            recv_sem=recv_sems.at[i],
            device_id=(moved(me, axis, offset), f),
            device_id_type=MESH,
        )
        copy.start()
        remote_copies.append(copy)
        return copy

    def local(src, dst):
        i = used[1]
        used[1] += 1
        copy = pltpu.make_async_copy(src, dst, local_sems.at[i])
        copy.start()
        local_copies.append(copy)
        return copy

    def own(t):
        return hist.at[:, pl.ds(SLICE * t, SLICE), :]

    barrier = pltpu.get_barrier_semaphore()
    partners = [(X, 1), (X, 2), (X, 3), (Y, 1), (Y, 2), (Y, 3), (Z, 1), (Z, 7)]
    for axis, offset in partners:
        pl.semaphore_signal(
            barrier, inc=1, device_id=(moved(me, axis, offset), f), device_id_type=MESH
        )
    pl.semaphore_wait(barrier, len(partners))

    z_in = {}
    mid_in = {}
    for t in (0, 1):
        for d in (1, -1):
            z_in[t, d] = remote(own(t), sets[t][0].at[d % 8], Z, d)
    for t in (2, 3):
        a = KINDS[t][0]
        for d in (1, -1):
            mid_in[t, d] = remote(own(t), sets[t][0].at[d % 4], a, d)
    for t in (0, 1):
        b = KINDS[t][1]
        for d in (1, -1):
            mid_in[t, d, 0] = remote(own(t), sets[t][d % 4].at[0], b, d)
    list_in = []
    for i, axis in enumerate((X, Y)):
        for k in (1, 2, 3):
            list_in.append(remote(plist, lists_v.at[3 * i + k], axis, -k))
    for t in range(4):
        sets[t][0][0] = hist[:, SLICE * t : SLICE * (t + 1), :]
    lists_v[0] = plist[...]

    def half_forward_first(t):
        a = KINDS[t][0]
        ring = sets[t][0]
        mid_in[t, 1].wait_recv()
        p = remote(ring.at[1, pl.ds(0, 4)], ring.at[2, pl.ds(0, 4)], a, 1)
        mid_in[t, -1].wait_recv()
        q = remote(ring.at[3, pl.ds(4, 4)], ring.at[2, pl.ds(4, 4)], a, -1)
        mid_in[t, 2] = (p, q)

    reach = {0: (3, 4), 1: (4, 3), 2: (4, 3), 3: (3, 4)}

    def z_arrival(t, h):
        z_in[t, h].wait_recv()
        d = 1 if h > 0 else -1
        limit = reach[t][0] if h > 0 else reach[t][1]
        here = sets[t][0].at[h % 8]
        if abs(h) < limit:
            z_in[t, h + d] = remote(here, sets[t][0].at[(h + d) % 8], Z, d)
        for e in (1, -1):
            mid_in[t, e, h] = remote(here, sets[t][e % 4].at[h % 8], KINDS[t][1], e)

    def half_forward(t, h):
        b = KINDS[t][1]
        mid_in[t, 1, h].wait_recv()
        p = remote(
            sets[t][1].at[h % 8, pl.ds(0, 4)], sets[t][2].at[h % 8, pl.ds(0, 4)], b, 1
        )
        mid_in[t, -1, h].wait_recv()
        q = remote(
            sets[t][3].at[h % 8, pl.ds(4, 4)], sets[t][2].at[h % 8, pl.ds(4, 4)], b, -1
        )
        mid_in[t, 2, h] = (p, q)

    wide_in = {}

    def wide_start(t):
        for copy in mid_in[t, 2]:
            copy.wait_recv()
        for d in (1, -1):
            wide_in[t, d] = remote(sets[t][0], sets[t][d % 8], Z, d)

    def wide_arrival(t, h):
        wide_in[t, h].wait_recv()
        d = 1 if h > 0 else -1
        limit = reach[t][0] if h > 0 else reach[t][1]
        if abs(h) < limit:
            wide_in[t, h + d] = remote(sets[t][h % 8], sets[t][(h + d) % 8], Z, d)

    last_in = []

    def pack(t, g):
        a, b, c = KINDS[t]
        n = SIZES[a]
        source = sets[t][g]
        target = packs[t]
        fixed = lax.rem(me[b] - g + SIZES[b], SIZES[b])

        def one(j, carry):
            there = lax.rem(me[a] - j + n, n)
            owner = me[c] * STRIDES[c] + fixed * STRIDES[b] + there * STRIDES[a]
            for k in range(4):
                slot = 0 if k == 0 else (k if c == X else 3 + k)
                for s in range(2):
                    index = jnp.clip(lists_s[slot, s, owner], 0, NB - 1)
                    target[k, g, there, s] = source[j, index]
            return carry

        lax.fori_loop(0, n, one, 0)
        where = [None, None, None]
        where[c] = me[c]
        where[b] = fixed
        where[a] = slice(None)
        spot = pulled.at[
            where[0], where[1], where[2], :, pl.ds(SLICE * t, SLICE), :
        ]
        for k in (1, 3, 2):
            last_in.append(remote(target.at[k, g], spot, c, k))
        local(target.at[0, g], spot)

    half_forward_first(2)
    half_forward_first(3)
    for h in (1, -1):
        for t in (0, 1):
            z_arrival(t, h)
    wide_start(2)
    wide_start(3)
    half_forward(0, 0)
    half_forward(1, 0)
    for copy in list_in:
        copy.wait_recv()
    fetch = local(lists_v, lists_s)
    fetch.wait()
    local_copies.remove(fetch)
    pack(2, 0)
    pack(3, 0)
    for s in (2, 3):
        for h in (s, -s):
            for t in (0, 1):
                z_arrival(t, h)
        for h in (s - 1, 1 - s):
            for t in (0, 1):
                half_forward(t, h)
    z_arrival(0, -4)
    z_arrival(1, 4)
    for h in (3, -3):
        for t in (0, 1):
            half_forward(t, h)
    wide_arrival(2, 1)
    wide_arrival(3, 1)
    wide_arrival(2, -1)
    wide_arrival(3, -1)
    half_forward(0, -4)
    half_forward(1, 4)
    for t in (0, 1):
        pack(t, 0)
    for t in (0, 1):
        pack(t, 1)
        pack(t, 3)
    for t in (0, 1):
        for h in (0, 1, -1, 2, -2, 3, -3, (-4, 4)[t]):
            for copy in mid_in[t, 2, h]:
                copy.wait_recv()
        pack(t, 2)
    for g in (1, 7):
        pack(2, g)
        pack(3, g)
    for s in (2, 3):
        for h in (s, -s):
            for t in (2, 3):
                wide_arrival(t, h)
                pack(t, h % 8)
    wide_arrival(2, 4)
    wide_arrival(3, -4)
    pack(2, 4)
    pack(3, 4)

    for copy in last_in:
        copy.wait_recv()
    for copy in local_copies:
        copy.wait()
    for copy in remote_copies:
        copy.wait_send()


def pull_blocks(blocks, plist):
    chunk8 = pltpu.VMEM((8, NB, SLICE, HALF), jnp.bfloat16)
    chunk4 = pltpu.VMEM((4, NB, SLICE, HALF), jnp.bfloat16)
    return pl.pallas_call(
        pull_kernel,
        out_shape=jax.ShapeDtypeStruct((4, 4, 8, 2, BLK, HALF), jnp.bfloat16),
        in_specs=[pl.BlockSpec(memory_space=pltpu.VMEM)] * 2,
        out_specs=pl.BlockSpec(memory_space=pl.ANY),
        scratch_shapes=[chunk8] * 8
        + [chunk4] * 16
        + [pltpu.VMEM((4, 4, 8, 2, SLICE, HALF), jnp.bfloat16)] * 2
        + [pltpu.VMEM((4, 8, 4, 2, SLICE, HALF), jnp.bfloat16)] * 2
        + [
            pltpu.VMEM((7, 2, 128), jnp.int32),
            pltpu.SMEM((7, 2, 128), jnp.int32),
            pltpu.SemaphoreType.DMA((192,)),
            pltpu.SemaphoreType.DMA((192,)),
            pltpu.SemaphoreType.DMA((32,)),
        ],
        compiler_params=pltpu.CompilerParams(
            collective_id=0, has_side_effects=True, vmem_limit_bytes=48 << 20
        ),
        name="pull_blocks",
    )(blocks, plist)


OWNERS_STEP = 8
STEPS = 128 // OWNERS_STEP
LOCAL_STEP = 64 // STEPS


def sum_kernel(
    plist, rdst, lsrc, ldst, pulled, rtiles, ltiles, hist, mine, following, acc
):
    i = pl.program_id(0)

    @pl.when(i == 0)
    def _():
        acc[...] = jnp.zeros_like(acc)

    terms = []
    for j in range(OWNERS_STEP):
        for c in range(2):
            o = i * OWNERS_STEP + j
            row = jnp.where(plist[c, o] >= 0, rdst[c, o], 2 * NB)
            terms.append(
                (
                    row,
                    jnp.dot(
                        rtiles[j, c], pulled[j, c], preferred_element_type=jnp.float32
                    ),
                )
            )
    for j in range(LOCAL_STEP):
        k = i * LOCAL_STEP + j
        terms.append(
            (
                ldst[0, k],
                jnp.dot(ltiles[j], hist[lsrc[0, k]], preferred_element_type=jnp.float32),
            )
        )
    for row, value in terms:
        acc[row] += value

    @pl.when(i == STEPS - 1)
    def _():
        mine[...] = acc[0:NB]
        following[...] = acc[NB : 2 * NB].astype(jnp.bfloat16)


def sum_tiles(plist, rdst, lsrc, ldst, pulled, rtiles, ltiles, blocks):
    pair = pl.BlockSpec((OWNERS_STEP, 2, BLK, BLK), lambda i, *_: (i, 0, 0, 0))
    return pl.pallas_call(
        sum_kernel,
        out_shape=(
            jax.ShapeDtypeStruct((NB, BLK, HALF), jnp.float32),
            jax.ShapeDtypeStruct((NB, BLK, HALF), jnp.bfloat16),
        ),
        grid_spec=pltpu.PrefetchScalarGridSpec(
            num_scalar_prefetch=4,
            grid=(STEPS,),
            in_specs=[
                pair,
                pair,
                pl.BlockSpec((LOCAL_STEP, BLK, BLK), lambda i, *_: (i, 0, 0)),
                pl.BlockSpec((NB, BLK, HALF), lambda i, *_: (0, 0, 0)),
            ],
            out_specs=[
                pl.BlockSpec((NB, BLK, HALF), lambda i, *_: (0, 0, 0)),
                pl.BlockSpec((NB, BLK, HALF), lambda i, *_: (0, 0, 0)),
            ],
            scratch_shapes=[pltpu.VMEM((2 * NB + 1, BLK, HALF), jnp.float32)],
        ),
        name="sum_tiles",
    )(plist, rdst, lsrc, ldst, pulled, rtiles, ltiles, blocks)


PIECE = 40
ROOT = 0.7978845608028654
CUBIC = 0.044715


def layer_kernel(
    mine,
    following,
    weight,
    bias,
    cotangent,
    new_rows,
    grad_weight,
    grad_bias,
    coming,
    agg,
    other,
    terms,
    z_part,
    plane,
    final,
    send_sems,
    recv_sems,
):
    me, f = coords()
    p = lax.axis_index("dom")
    used = [0]
    copies = []

    def remote(src, dst, dom, feat):
        i = used[0]
        used[0] += 1
        copy = pltpu.make_async_remote_copy(
            src_ref=src,
            dst_ref=dst,
            send_sem=send_sems.at[i],
            recv_sem=recv_sems.at[i],
            device_id=(dom, feat),
            device_id_type=MESH,
        )
        copy.start()
        copies.append(copy)
        return copy

    up = lax.rem(p + 1, 128)
    down = lax.rem(p + 127, 128)
    column = [moved(me, Z, k) for k in range(1, 8)]
    flat = [
        lax.rem(me[0] + i, 4) * 32 + lax.rem(me[1] + j, 4) * 8 + me[2]
        for i in range(4)
        for j in range(4)
        if i or j
    ]
    barrier = pltpu.get_barrier_semaphore()
    greeted = [(up, f), (down, f), (p, 1 - f)] + [(d, f) for d in column + flat]
    for d in greeted:
        pl.semaphore_signal(barrier, inc=1, device_id=d, device_id_type=MESH)
    pl.semaphore_wait(barrier, len(greeted))

    shifts = [remote(following.at[t], coming.at[t], up, f) for t in range(NB)]
    swaps = []
    for t in range(NB):
        shifts[t].wait_recv()
        agg[t] = (mine[t] + coming[t].astype(jnp.float32)).astype(jnp.bfloat16)
        swaps.append(remote(agg.at[t], other.at[t], p, 1 - f))
    w_mine = weight[pl.ds(pl.multiple_of(f * HALF, HALF), HALF), :]
    w_other = weight[pl.ds(pl.multiple_of((1 - f) * HALF, HALF), HALF), :]
    b = bias[...]
    g_mine = jnp.zeros((HALF, HALF), jnp.float32)
    g_other = jnp.zeros((HALF, HALF), jnp.float32)
    g_bias = jnp.zeros((8, HALF), jnp.float32)
    for t in range(NB):
        swaps[t].wait_recv()
        a0 = agg[t]
        a1 = other[t]
        v = (
            jnp.dot(a0, w_mine, preferred_element_type=jnp.float32)
            + jnp.dot(a1, w_other, preferred_element_type=jnp.float32)
            + b
        )
        v2 = v * v
        th = jnp.tanh(ROOT * (v + CUBIC * (v2 * v)))
        half = 0.5 * (1.0 + th)
        rows = slice(BLK * t, BLK * (t + 1))
        new_rows[rows, :] = (v * half).astype(jnp.bfloat16)
        slope = half + (0.5 * ROOT) * v * (1.0 - th * th) * (1.0 + (3.0 * CUBIC) * v2)
        gp = (cotangent[rows, :].astype(jnp.float32) * slope).astype(jnp.bfloat16)
        dims = (((0,), (0,)), ((), ()))
        g_mine += lax.dot_general(a0, gp, dims, preferred_element_type=jnp.float32)
        g_other += lax.dot_general(a1, gp, dims, preferred_element_type=jnp.float32)
        g_bias += jnp.sum(gp.astype(jnp.float32).reshape(16, 8, HALF), axis=0)
    terms[pl.ds(f * 4, 4), 0:32, :] = g_mine.reshape(4, 32, HALF)
    terms[pl.ds((1 - f) * 4, 4), 0:32, :] = g_other.reshape(4, 32, HALF)
    terms[:, 32:40, :] = jnp.zeros((8, 8, HALF), jnp.float32)
    terms[0, 32:40, :] = g_bias

    ins = []
    for k in range(1, 8):
        there = lax.rem(me[2] + k, 8)
        ins.append(remote(terms.at[there], z_part.at[k - 1], column[k - 1], f))
    total = terms[me[2]]
    for k in range(7):
        ins[k].wait_recv()
        total = total + z_part[k]
    spot = me[0] * 4 + me[1]
    plane[spot] = total
    ins = [remote(plane.at[spot], plane.at[spot], d, f) for d in flat]
    for copy in ins:
        copy.wait_recv()
    total = plane[0]
    for k in range(1, 16):
        total = total + plane[k]
    final[me[2]] = total
    ins = [remote(final.at[me[2]], final.at[me[2]], d, f) for d in column]
    for copy in ins:
        copy.wait_recv()
    for k in range(8):
        grad_weight[32 * k : 32 * (k + 1), :] = final[k, 0:32, :]
    grad_bias[...] = jnp.sum(final[0, 32:40, :], axis=0, keepdims=True)
    for copy in copies:
        copy.wait_send()


def layer(mine, following, weight, bias, cotangent):
    vm = pl.BlockSpec(memory_space=pltpu.VMEM)
    return pl.pallas_call(
        layer_kernel,
        out_shape=(
            jax.ShapeDtypeStruct((NB * BLK, HALF), jnp.bfloat16),
            jax.ShapeDtypeStruct((2 * HALF, HALF), jnp.float32),
            jax.ShapeDtypeStruct((1, HALF), jnp.float32),
        ),
        in_specs=[vm] * 5,
        out_specs=(vm, vm, vm),
        scratch_shapes=[
            pltpu.VMEM((NB, BLK, HALF), jnp.bfloat16),
            pltpu.VMEM((NB, BLK, HALF), jnp.bfloat16),
            pltpu.VMEM((NB, BLK, HALF), jnp.bfloat16),
            pltpu.VMEM((8, PIECE, HALF), jnp.float32),
            pltpu.VMEM((7, PIECE, HALF), jnp.float32),
            pltpu.VMEM((16, PIECE, HALF), jnp.float32),
            pltpu.VMEM((8, PIECE, HALF), jnp.float32),
            pltpu.SemaphoreType.DMA((48,)),
            pltpu.SemaphoreType.DMA((48,)),
        ],
        compiler_params=pltpu.CompilerParams(
            collective_id=1, has_side_effects=True, vmem_limit_bytes=32 << 20
        ),
        name="layer",
    )(mine, following, weight, bias, cotangent)


def per_device(
    history,
    pull_list,
    remote_tiles,
    remote_dst,
    local_tiles,
    local_src,
    local_dst,
    weight,
    bias,
    cotangent,
):
    blocks = history.reshape(NB, BLK, HALF)
    plist = pull_list[0].T
    pulled = pull_blocks(blocks, plist)
    mine, following = sum_tiles(
        plist,
        remote_dst[0].T,
        local_src,
        local_dst,
        pulled.reshape(128, 2, BLK, HALF),
        remote_tiles[0],
        local_tiles,
        blocks,
    )
    new_rows, grad_weight, grad_bias = layer(
        mine, following, weight, bias.reshape(1, HALF), cotangent
    )
    return new_rows, grad_weight, grad_bias.reshape(HALF)


def solution(mesh):
    placed = (
        P("dom", "feat"),
        P("dom", None, None),
        P("dom", None, None, None, None),
        P("dom", None, None),
        P("dom", None, None),
        P("dom", None),
        P("dom", None),
        P(None, "feat"),
        P("feat"),
        P("dom", "feat"),
    )
    return jax.shard_map(
        per_device,
        mesh=mesh,
        in_specs=placed,
        out_specs=(P("dom", "feat"), P(None, "feat"), P("feat")),
        check_vma=False,
    )
```

```python
import functools

import jax
import jax.numpy as jnp
from jax import lax
from jax.sharding import PartitionSpec as P
from jax.experimental import pallas as pl
from jax.experimental.pallas import tpu as pltpu

MESH = pl.DeviceIdType.MESH
X, Y, Z = 0, 1, 2
SIZES = (4, 4, 8)
STRIDES = (32, 8, 1)
NB = 8
BLK = 128
HALF = 128
SLICE = 32
KINDS = ((Z, Y, X), (Z, X, Y), (Y, Z, X), (X, Z, Y))


def coords():
    p = lax.axis_index("dom")
    return (p // 32, lax.rem(p // 8, 4), lax.rem(p, 8)), lax.axis_index("feat")


def group_rank(h):
    return jnp.where(h == 0, 0, jnp.where(h <= 4, 2 * h - 1, 2 * (8 - h)))


def moved(me, axis, offset):
    n = SIZES[axis]
    there = list(me)
    there[axis] = lax.rem(me[axis] + (offset % n), n)
    return there[0] * 32 + there[1] * 8 + there[2]


PIECE = 24
ROOT = 0.7978845608028654
CUBIC = 0.044715
TILES = 320
LOCAL = 64


def step_kernel(
    history,
    table,
    rtiles,
    ltiles,
    cotangent,
    weight,
    bias,
    new_rows,
    grad_weight,
    grad_bias,
    *scratch,
):
    sets = [scratch[0:4], scratch[4:8], scratch[8:16], scratch[16:24]]
    packs = scratch[24:28]
    (
        lists_v,
        lists_s,
        hist,
        rt,
        lt,
        cot,
        pulled,
        sums,
        following,
        coming,
        agg,
        other,
        terms,
        part,
        column_sums,
        final,
        send_sems,
        recv_sems,
        local_sems,
    ) = scratch[28:]
    me, f = coords()
    p = lax.axis_index("dom")
    used = [0, 0]
    remote_copies = []

    def send(src, dst, dom, feat):
        i = used[0]
        used[0] += 1
        copy = pltpu.make_async_remote_copy(
            src_ref=src,
            dst_ref=dst,
            send_sem=send_sems.at[i],
            recv_sem=recv_sems.at[i],
            device_id=(dom, feat),
            device_id_type=MESH,
        )
        copy.start()
        remote_copies.append(copy)
        return copy

    def remote(src, dst, axis, offset):
        return send(src, dst, moved(me, axis, offset), f)

    def local(src, dst):
        i = used[1]
        used[1] += 1
        copy = pltpu.make_async_copy(src, dst, local_sems.at[i])
        copy.start()
        return copy

    def own(t):
        return hist.at[:, pl.ds(SLICE * t, SLICE), :]

    load_hist = local(history, hist)
    up = lax.rem(p + 1, 128)
    down = lax.rem(p + 127, 128)
    column = [moved(me, Z, k) for k in range(1, 8)]
    flat = [
        lax.rem(me[0] + i, 4) * 32 + lax.rem(me[1] + j, 4) * 8 + me[2]
        for i in range(4)
        for j in range(4)
        if i or j
    ]
    barrier = pltpu.get_barrier_semaphore()
    greeted = [(up, f), (down, f), (p, 1 - f)] + [(d, f) for d in column + flat]
    for d in greeted:
        pl.semaphore_signal(barrier, inc=1, device_id=d, device_id_type=MESH)
    load_rt = local(rtiles, rt)
    load_lt = local(ltiles, lt)
    load_cot = local(cotangent, cot)
    sums[TILES] = jnp.zeros((BLK, HALF), jnp.float32)
    load_hist.wait()
    pl.semaphore_wait(barrier, len(greeted))

    z_in = {}
    mid_in = {}
    wide_in = {}
    last_in = {}
    list_in = []
    reach = {0: (3, 4), 1: (4, 3), 2: (4, 3), 3: (3, 4)}

    def z_start(t):
        for d in (1, -1):
            z_in[t, d] = remote(own(t), sets[t][0].at[d % 8], Z, d)

    def first_start(t):
        for d in (1, -1):
            mid_in[t, d] = remote(own(t), sets[t][0].at[d % 4], KINDS[t][0], d)

    def mid_start(t):
        for d in (1, -1):
            mid_in[t, d, 0] = remote(own(t), sets[t][d % 4].at[0], KINDS[t][1], d)

    def lists_start():
        for i, axis in enumerate((X, Y)):
            for k in (1, 2, 3):
                list_in.append(remote(table, lists_v.at[3 * i + k], axis, -k))

    def lists_end():
        for copy in list_in:
            copy.wait_recv()
        local(lists_v, lists_s).wait()

    def half_forward_first(t):
        a = KINDS[t][0]
        ring = sets[t][0]
        mid_in[t, 1].wait_recv()
        u = remote(ring.at[1, pl.ds(0, 4)], ring.at[2, pl.ds(0, 4)], a, 1)
        mid_in[t, -1].wait_recv()
        v = remote(ring.at[3, pl.ds(4, 4)], ring.at[2, pl.ds(4, 4)], a, -1)
        mid_in[t, 2] = (u, v)

    def first_end(t):
        for copy in mid_in[t, 2]:
            copy.wait_recv()

    def z_arrival(t, h):
        z_in[t, h].wait_recv()
        d = 1 if h > 0 else -1
        limit = reach[t][0] if h > 0 else reach[t][1]
        here = sets[t][0].at[h % 8]
        if abs(h) < limit:
            z_in[t, h + d] = remote(here, sets[t][0].at[(h + d) % 8], Z, d)
        for e in (1, -1):
            mid_in[t, e, h] = remote(here, sets[t][e % 4].at[h % 8], KINDS[t][1], e)

    def half_forward(t, h):
        b = KINDS[t][1]
        s = h % 8
        mid_in[t, 1, h].wait_recv()
        u = remote(sets[t][1].at[s, pl.ds(0, 4)], sets[t][2].at[s, pl.ds(0, 4)], b, 1)
        mid_in[t, -1, h].wait_recv()
        v = remote(sets[t][3].at[s, pl.ds(4, 4)], sets[t][2].at[s, pl.ds(4, 4)], b, -1)
        mid_in[t, 2, h] = (u, v)

    def half_end(t):
        for h in (0, 1, -1, 2, -2, 3, -3, (-4, 4)[t]):
            for copy in mid_in[t, 2, h]:
                copy.wait_recv()

    def wide_start(t, q):
        source = own(t) if q == 0 else sets[t][0].at[q]
        for d in (1, -1):
            wide_in[t, d, q] = remote(source, sets[t][d % 8].at[q], Z, d)

    def wide_arrival(t, h, q):
        if (t, h, q) not in wide_in:
            return
        wide_in[t, h, q].wait_recv()
        d = 1 if h > 0 else -1
        limit = reach[t][0] if h > 0 else reach[t][1]
        if abs(h) < limit:
            wide_in[t, h + d, q] = remote(
                sets[t][h % 8].at[q], sets[t][(h + d) % 8].at[q], Z, d
            )

    def pack(t, g):
        a, b, c = KINDS[t]
        n = SIZES[a]
        source = sets[t][g]
        target = packs[t]
        fixed = lax.rem(me[b] - g + SIZES[b], SIZES[b])
        rows = pl.ds(SLICE * t, SLICE)

        def spot(there, *rest):
            where = [None, None, None]
            where[c] = me[c]
            where[b] = fixed
            where[a] = there
            return (where[0], where[1], where[2]) + rest

        def one(j, carry):
            there = lax.rem(me[a] - j + n, n)
            owner = me[c] * STRIDES[c] + fixed * STRIDES[b] + there * STRIDES[a]
            for k in range(4):
                slot = 0 if k == 0 else (k if c == X else 3 + k)
                for s in range(2):
                    index = jnp.clip(lists_s[slot, s, owner], 0, NB - 1)
                    value = source[j, index]
                    if k == 0:
                        pulled[spot(there, s, rows, slice(None))] = value
                    else:
                        target[k - 1, g, there, s] = value
            return carry

        lax.fori_loop(0, n, one, 0)
        to = pulled.at[spot(slice(None), slice(None), rows, slice(None))]
        last_in[t, g] = [remote(target.at[k - 1, g], to, c, k) for k in (1, 3, 2)]

    def arrived(t, g):
        for copy in last_in[t, g]:
            copy.wait_recv()

    def local_tiles(start, stop):
        def eight(i, carry):
            values = []
            for j in range(8):
                k = i * 8 + j
                values.append(
                    jnp.dot(
                        lt[k], hist[lists_s[0, 5, k]], preferred_element_type=jnp.float32
                    )
                )
            for j in range(8):
                k = i * 8 + j
                sums[k] = sums[lists_s[0, 4, k]] + values[j]
            return carry

        lax.fori_loop(start, stop, eight, 0)

    order = (0, 1, 7, 2, 6, 3, 5, 4)

    def remote_tiles(g):
        first = LOCAL + 32 * order.index(g)
        z = lax.rem(me[2] - g + 8, 8)

        def eight(i, carry):
            values = []
            for j in range(4):
                o = i * 32 + j * 8 + z
                for c in range(2):
                    values.append(
                        jnp.dot(
                            rt[o, c], pulled[i, j, z, c], preferred_element_type=jnp.float32
                        )
                    )
            for j in range(4):
                o = i * 32 + j * 8 + z
                for c in range(2):
                    sums[first + i * 8 + j * 2 + c] = (
                        sums[lists_s[0, 2 + c, o]] + values[2 * j + c]
                    )
            return carry

        lax.fori_loop(0, 4, eight, 0)


    z_start(0)
    z_start(1)
    first_start(2)
    first_start(3)
    lists_start()
    mid_start(0)
    mid_start(1)
    for t in range(4):
        sets[t][0][0] = hist[:, SLICE * t : SLICE * (t + 1), :]
    lists_v[0] = table[...]
    wide_start(2, 0)
    wide_start(3, 0)
    half_forward_first(2)
    half_forward_first(3)
    for h in (1, -1):
        for t in (0, 1):
            z_arrival(t, h)
    half_forward(0, 0)
    half_forward(1, 0)
    lists_end()
    first_end(2)
    first_end(3)
    pack(2, 0)
    pack(3, 0)
    wide_start(2, 1)
    wide_start(3, 1)
    for h in (2, -2):
        for t in (0, 1):
            z_arrival(t, h)
    for h in (1, -1):
        for t in (0, 1):
            half_forward(t, h)
    wide_start(2, 3)
    wide_start(3, 3)
    for h in (3, -3):
        for t in (0, 1):
            z_arrival(t, h)
    wide_start(2, 2)
    wide_start(3, 2)
    for h in (1, -1):
        for t in (2, 3):
            wide_arrival(t, h, 0)
    for h in (2, -2):
        for t in (0, 1):
            half_forward(t, h)
    for h in (1, -1):
        for t in (2, 3):
            wide_arrival(t, h, 1)
    z_arrival(0, -4)
    z_arrival(1, 4)
    for h in (3, -3):
        for t in (0, 1):
            half_forward(t, h)
    pack(0, 0)
    pack(1, 0)
    for h in (1, -1):
        for t in (2, 3):
            wide_arrival(t, h, 3)
    half_forward(0, -4)
    half_forward(1, 4)
    for g in (1, 3):
        pack(0, g)
        pack(1, g)
    for h in (1, -1):
        for t in (2, 3):
            wide_arrival(t, h, 2)
    for g in (1, 7):
        pack(2, g)
        pack(3, g)
    for t in (0, 1):
        half_end(t)
        pack(t, 2)
    load_lt.wait()
    for s in (2, 3, 4):
        for i, q in enumerate((0, 1, 3, 2)):
            for h in (s, -s):
                for t in (2, 3):
                    wide_arrival(t, h, q)
            if s == 2:
                local_tiles(2 * i, 2 * i + 2)
        for h in (s, -s):
            for t in (2, 3):
                if (t, h, 0) in wide_in:
                    pack(t, h % 8)
    load_rt.wait()
    for t in (0, 1):
        for g in (0, 1, 3, 2):
            arrived(t, g)
    for g in order:
        arrived(2, g)
        arrived(3, g)
        remote_tiles(g)

    load_cot.wait()
    shifts = []
    for t in range(NB):
        following[t] = sums[lists_s[0, 4, 64 + NB + t]].astype(jnp.bfloat16)
        shifts.append(send(following.at[t], coming.at[t], up, f))
    swaps = []
    for t in range(NB):
        mine = sums[lists_s[0, 4, 64 + t]]
        shifts[t].wait_recv()
        agg[t] = (mine + coming[t].astype(jnp.float32)).astype(jnp.bfloat16)
        swaps.append(send(agg.at[t], other.at[t], p, 1 - f))
    w_mine = weight[pl.ds(pl.multiple_of(f * HALF, HALF), HALF), :]
    w_other = weight[pl.ds(pl.multiple_of((1 - f) * HALF, HALF), HALF), :]
    b = bias[...]
    g_mine = jnp.zeros((HALF, HALF), jnp.float32)
    g_other = jnp.zeros((HALF, HALF), jnp.float32)
    g_bias = jnp.zeros((8, HALF), jnp.float32)
    for t in range(NB):
        swaps[t].wait_recv()
        a0 = agg[t]
        a1 = other[t]
        v = (
            jnp.dot(a0, w_mine, preferred_element_type=jnp.float32)
            + jnp.dot(a1, w_other, preferred_element_type=jnp.float32)
            + b
        )
        v2 = v * v
        th = jnp.tanh(ROOT * (v + CUBIC * (v2 * v)))
        half = 0.5 * (1.0 + th)
        rows = slice(BLK * t, BLK * (t + 1))
        new_rows[rows, :] = (v * half).astype(jnp.bfloat16)
        slope = half + (0.5 * ROOT) * v * (1.0 - th * th) * (1.0 + (3.0 * CUBIC) * v2)
        gp = (cot[rows, :].astype(jnp.float32) * slope).astype(jnp.bfloat16)
        dims = (((0,), (0,)), ((), ()))
        g_mine += lax.dot_general(a0, gp, dims, preferred_element_type=jnp.float32)
        g_other += lax.dot_general(a1, gp, dims, preferred_element_type=jnp.float32)
        g_bias += jnp.sum(gp.astype(jnp.float32).reshape(16, 8, HALF), axis=0)
    terms[pl.ds(f * 8, 8), 0:16, :] = g_mine.reshape(8, 16, HALF)
    terms[pl.ds((1 - f) * 8, 8), 0:16, :] = g_other.reshape(8, 16, HALF)
    terms[:, 16:24, :] = jnp.zeros((16, 8, HALF), jnp.float32)
    terms[0, 16:24, :] = g_bias

    spot = me[0] * 4 + me[1]
    ins = [send(terms.at[d // 8], part.at[i], d, f) for i, d in enumerate(flat)]
    total = terms[spot]
    for i in range(15):
        ins[i].wait_recv()
        total = total + part[i]
    column_sums[me[2]] = total
    ins = [send(column_sums.at[me[2]], column_sums.at[me[2]], d, f) for d in column]
    for copy in ins:
        copy.wait_recv()
    total = column_sums[0]
    for k in range(1, 8):
        total = total + column_sums[k]
    final[spot] = total
    ins = [send(final.at[spot], final.at[spot], d, f) for d in flat]
    for copy in ins:
        copy.wait_recv()
    for k in range(16):
        grad_weight[16 * k : 16 * (k + 1), :] = final[k, 0:16, :]
    grad_bias[...] = jnp.sum(final[0, 16:24, :], axis=0, keepdims=True)
    for copy in remote_copies:
        copy.wait_send()


def step(blocks, table, rtiles, ltiles, cotangent, weight, bias):
    vm = pl.BlockSpec(memory_space=pltpu.VMEM)
    hbm = pl.BlockSpec(memory_space=pl.ANY)
    bf16 = jnp.bfloat16
    f32 = jnp.float32
    return pl.pallas_call(
        step_kernel,
        out_shape=(
            jax.ShapeDtypeStruct((NB * BLK, HALF), bf16),
            jax.ShapeDtypeStruct((2 * HALF, HALF), f32),
            jax.ShapeDtypeStruct((1, HALF), f32),
        ),
        in_specs=[hbm, vm, hbm, hbm, hbm, vm, vm],
        out_specs=(vm, vm, vm),
        scratch_shapes=[pltpu.VMEM((8, NB, SLICE, HALF), bf16)] * 8
        + [pltpu.VMEM((4, NB, SLICE, HALF), bf16)] * 16
        + [pltpu.VMEM((3, 4, 8, 2, SLICE, HALF), bf16)] * 2
        + [pltpu.VMEM((3, 8, 4, 2, SLICE, HALF), bf16)] * 2
        + [
            pltpu.VMEM((7, 8, 128), jnp.int32),
            pltpu.SMEM((7, 8, 128), jnp.int32),
            pltpu.VMEM((NB, BLK, HALF), bf16),
            pltpu.VMEM((128, 2, BLK, BLK), bf16),
            pltpu.VMEM((LOCAL, BLK, BLK), bf16),
            pltpu.VMEM((NB * BLK, HALF), bf16),
            pltpu.VMEM((4, 4, 8, 2, BLK, HALF), bf16),
            pltpu.VMEM((TILES + 1, BLK, HALF), f32),
            pltpu.VMEM((NB, BLK, HALF), bf16),
            pltpu.VMEM((NB, BLK, HALF), bf16),
            pltpu.VMEM((NB, BLK, HALF), bf16),
            pltpu.VMEM((NB, BLK, HALF), bf16),
            pltpu.VMEM((16, PIECE, HALF), f32),
            pltpu.VMEM((15, PIECE, HALF), f32),
            pltpu.VMEM((8, PIECE, HALF), f32),
            pltpu.VMEM((16, PIECE, HALF), f32),
            pltpu.SemaphoreType.DMA((320,)),
            pltpu.SemaphoreType.DMA((320,)),
            pltpu.SemaphoreType.DMA((8,)),
        ],
        compiler_params=pltpu.CompilerParams(
            collective_id=0, has_side_effects=True, vmem_limit_bytes=67043328
        ),
        name="step",
    )(blocks, table, rtiles, ltiles, cotangent, weight, bias)


def index_table(plist, remote_dst, local_src, local_dst):
    mz = lax.rem(lax.axis_index("dom"), 8)
    i = jnp.arange(256, dtype=jnp.int32)
    o = i // 2
    h = lax.rem(mz - lax.rem(o, 8) + 8, 8)
    key = LOCAL + group_rank(h) * 32 + (o // 32) * 8 + lax.rem(o // 8, 4) * 2 + lax.rem(i, 2)
    near = jnp.arange(LOCAL, dtype=jnp.int32)
    dst = jnp.where(plist.reshape(-1) >= 0, remote_dst.reshape(-1), -1)
    dst = jnp.concatenate([local_dst.reshape(-1), dst])
    keys = jnp.concatenate([near, key])
    want = jnp.concatenate(
        [remote_dst.T.reshape(-1), local_dst.reshape(-1), jnp.arange(16, dtype=jnp.int32)]
    )
    limit = jnp.concatenate(
        [key.reshape(128, 2).T.reshape(-1), near, jnp.full((16,), TILES, jnp.int32)]
    )
    match = (want[:, None] == dst[None, :]) & (keys[None, :] < limit[:, None])
    before = jnp.max(jnp.where(match, keys[None, :], -1), axis=1)
    before = jnp.where(before < 0, TILES, before)
    return jnp.concatenate(
        [
            plist.T.reshape(-1),
            before,
            jnp.zeros((48,), jnp.int32),
            local_src.reshape(-1),
            jnp.zeros((64 + 256,), jnp.int32),
        ]
    ).reshape(8, 128)


def per_device(
    history,
    pull_list,
    remote_tiles,
    remote_dst,
    local_tiles,
    local_src,
    local_dst,
    weight,
    bias,
    cotangent,
):
    table = index_table(pull_list[0], remote_dst[0], local_src, local_dst)
    new_rows, grad_weight, grad_bias = step(
        history.reshape(NB, BLK, HALF),
        table,
        remote_tiles[0],
        local_tiles,
        cotangent,
        weight,
        bias.reshape(1, HALF),
    )
    return new_rows, grad_weight, grad_bias.reshape(HALF)


def solution(mesh):
    placed = (
        P("dom", "feat"),
        P("dom", None, None),
        P("dom", None, None, None, None),
        P("dom", None, None),
        P("dom", None, None),
        P("dom", None),
        P("dom", None),
        P(None, "feat"),
        P("feat"),
        P("dom", "feat"),
    )
    return jax.shard_map(
        per_device,
        mesh=mesh,
        in_specs=placed,
        out_specs=(P("dom", "feat"), P(None, "feat"), P("feat")),
        check_vma=False,
    )
```

```python
import functools

import jax
import jax.numpy as jnp
from jax import lax
from jax.sharding import PartitionSpec as P
from jax.experimental import pallas as pl
from jax.experimental.pallas import tpu as pltpu

MESH = pl.DeviceIdType.MESH
X, Y, Z = 0, 1, 2
SIZES = (4, 4, 8)
STRIDES = (32, 8, 1)
NB = 8
BLK = 128
HALF = 128
SLICE = 32
KINDS = ((Z, Y, X), (Z, X, Y), (Y, Z, X), (X, Z, Y))


def coords():
    p = lax.axis_index("dom")
    return (p // 32, lax.rem(p // 8, 4), lax.rem(p, 8)), lax.axis_index("feat")


def group_rank(h):
    return jnp.where(h == 0, 0, jnp.where(h <= 4, 2 * h - 1, 2 * (8 - h)))


def moved(me, axis, offset):
    n = SIZES[axis]
    there = list(me)
    there[axis] = lax.rem(me[axis] + (offset % n), n)
    return there[0] * 32 + there[1] * 8 + there[2]


PIECE = 24
ROOT = 0.7978845608028654
CUBIC = 0.044715
TILES = 320
LOCAL = 64
LAG = 2
SLOTS = 3
EVENTS = (
    ("s", 2, 0), ("z", 0, 1), ("z", 0, -1), ("f", 2, 1), ("f", 2, -1), ("f", 3, 1), ("f", 3, -1),
    ("z", 1, 1), ("z", 1, -1), ("m", 0, 1, 0), ("m", 0, -1, 0), ("m", 1, 1, 0), ("m", 1, -1, 0),
    ("w", 2, 1, 0), ("w", 2, -1, 0), ("m", 0, 1, 1), ("m", 0, -1, 1), ("m", 1, 1, 1), ("m", 1, -1, 1),
    ("p", 3, 0), ("z", 0, 2), ("z", 0, -2), ("m", 0, 1, -1), ("m", 0, -1, -1), ("p", 2, 0), ("m", 1, 1, -1),
    ("m", 1, -1, -1), ("z", 1, 2), ("z", 1, -2), ("w", 2, 2, 0), ("w", 2, -2, 0), ("z", 0, 3), ("z", 0, -3),
    ("s", 3, 0), ("z", 1, 3), ("z", 1, -3), ("m", 0, 1, 2), ("m", 0, -1, 2), ("w", 2, 3, 0), ("w", 2, -3, 0),
    ("s", 2, 1), ("m", 1, 1, 2), ("m", 1, -1, 2), ("m", 0, 1, -2), ("m", 0, -1, -2), ("w", 3, 1, 0),
    ("z", 0, -4), ("s", 2, 3), ("m", 1, 1, -2), ("m", 1, -1, -2), ("z", 1, 4), ("w", 3, -1, 0),
    ("m", 0, 1, 3), ("m", 0, -1, 3), ("m", 1, 1, 3), ("m", 1, -1, 3), ("w", 2, 4, 0), ("w", 2, -1, 1),
    ("m", 0, 1, -3), ("m", 0, -1, -3), ("m", 1, 1, -3), ("m", 1, -1, -3), ("w", 2, 1, 1), ("w", 2, -1, 3),
    ("p", 1, 0), ("p", 0, 0), ("w", 3, 2, 0), ("w", 3, -2, 0), ("m", 0, 1, -4), ("m", 0, -1, -4),
    ("m", 1, 1, 4), ("m", 1, -1, 4), ("w", 2, 1, 3), ("w", 2, -2, 1), ("w", 2, 2, 1), ("w", 2, -2, 3),
    ("w", 3, 3, 0), ("w", 3, -3, 0), ("s", 3, 1), ("p", 1, 1), ("w", 2, 2, 3), ("w", 2, -3, 1), ("p", 0, 1),
    ("w", 2, 3, 1), ("w", 2, -3, 3), ("s", 3, 3), ("w", 3, 1, 1), ("w", 3, -4, 0), ("s", 3, 2),
    ("w", 2, 3, 3), ("w", 3, -1, 1), ("p", 1, 3), ("p", 0, 3), ("s", 2, 2), ("w", 2, 4, 1), ("w", 3, -1, 3),
    ("w", 3, 1, 3), ("w", 3, -1, 2), ("w", 3, 2, 1), ("w", 3, -2, 1), ("w", 3, 1, 2), ("w", 2, -1, 2),
    ("p", 1, 2), ("p", 0, 2), ("w", 2, 4, 3), ("w", 3, -2, 3), ("w", 2, 1, 2), ("w", 3, -2, 2),
    ("w", 3, 2, 3), ("w", 3, -3, 1), ("w", 3, 3, 1), ("w", 2, -2, 2), ("p", 3, 7), ("w", 3, 2, 2),
    ("w", 3, -3, 3), ("p", 2, 7), ("w", 2, 2, 2), ("w", 3, -3, 2), ("p", 3, 1), ("w", 3, 3, 3),
    ("w", 3, -4, 1), ("p", 2, 1), ("w", 3, 3, 2), ("w", 2, -3, 2), ("p", 3, 6), ("w", 2, 3, 2),
    ("w", 3, -4, 3), ("p", 2, 6), ("w", 3, -4, 2), ("p", 3, 2), ("w", 2, 4, 2), ("p", 2, 2), ("p", 3, 5),
    ("p", 2, 5), ("p", 3, 3), ("p", 2, 3), ("p", 3, 4), ("p", 2, 4),
)


def step_kernel(
    history,
    plist,
    rdst,
    lsrc,
    ldst,
    rtiles,
    ltiles,
    cotangent,
    weight_hbm,
    bias_hbm,
    new_rows,
    grad_weight,
    grad_bias,
    *scratch,
):
    sets = [scratch[0:4], scratch[4:8], scratch[8:16], scratch[16:24]]
    packs = scratch[24:28]
    (
        lists_v,
        lists_s,
        rdst_v,
        ldst_v,
        lsrc_s,
        rows_v,
        rows_s,
        weight,
        bias,
        hist,
        rt,
        lt,
        cot,
        pulled,
        sums,
        following,
        coming,
        agg,
        other,
        terms,
        part,
        column_sums,
        final,
        send_sems,
        recv_sems,
        local_sems,
    ) = scratch[28:]
    me, f = coords()
    p = lax.axis_index("dom")
    used = [0, 0]
    remote_copies = []

    def send(src, dst, dom, feat):
        i = used[0]
        used[0] += 1
        copy = pltpu.make_async_remote_copy(
            src_ref=src,
            dst_ref=dst,
            send_sem=send_sems.at[i],
            recv_sem=recv_sems.at[i],
            device_id=(dom, feat),
            device_id_type=MESH,
        )
        copy.start()
        remote_copies.append(copy)
        return copy

    def remote(src, dst, axis, offset):
        return send(src, dst, moved(me, axis, offset), f)

    def local(src, dst):
        i = used[1]
        used[1] += 1
        copy = pltpu.make_async_copy(src, dst, local_sems.at[i])
        copy.start()
        return copy

    def own(t):
        return hist.at[:, pl.ds(SLICE * t, SLICE), :]

    load_hist = local(history, hist)
    small = [
        local(plist, lists_v.at[0]),
        local(rdst, rdst_v),
        local(ldst, ldst_v),
        local(lsrc, lsrc_s),
    ]
    up = lax.rem(p + 1, 128)
    down = lax.rem(p + 127, 128)
    column = [moved(me, Z, k) for k in range(1, 8)]
    flat = [
        lax.rem(me[0] + i, 4) * 32 + lax.rem(me[1] + j, 4) * 8 + me[2]
        for i in range(4)
        for j in range(4)
        if i or j
    ]
    barrier = pltpu.get_barrier_semaphore()
    greeted = [(up, f), (down, f), (p, 1 - f)] + [(d, f) for d in column + flat]
    for d in greeted:
        pl.semaphore_signal(barrier, inc=1, device_id=d, device_id_type=MESH)
    order = (0, 1, 7, 2, 6, 3, 5, 4)

    def load_tiles(i):
        z = lax.rem(me[2] - order[i] + 8, 8)
        return local(rtiles.at[:, :, z], rt.at[i % SLOTS])

    tiles_in = [load_tiles(i) for i in range(SLOTS)]
    load_lt = local(ltiles, lt)
    load_cot = local(cotangent, cot)
    load_weight = local(weight_hbm, weight)
    load_bias = local(bias_hbm, bias)
    sums[TILES] = jnp.zeros((BLK, HALF), jnp.float32)
    load_hist.wait()
    for copy in small:
        copy.wait()
    pl.semaphore_wait(barrier, len(greeted))

    z_in = {}
    mid_in = {}
    wide_in = {}
    far_in = {}
    last_in = {}
    list_in = []
    reach = {0: (3, 4), 1: (4, 3), 2: (4, 3), 3: (3, 4)}

    def z_start(t):
        for d in (1, -1):
            z_in[t, d] = remote(own(t), sets[t][0].at[d % 8], Z, d)

    def first_start(t):
        for d in (1, -1):
            mid_in[t, d] = remote(own(t), sets[t][0].at[d % 4], KINDS[t][0], d)

    def mid_start(t):
        for d in (1, -1):
            mid_in[t, d, 0] = remote(own(t), sets[t][d % 4].at[0], KINDS[t][1], d)

    def lists_start():
        for i, axis in enumerate((X, Y)):
            for k in (1, 2, 3):
                list_in.append(remote(lists_v.at[0], lists_v.at[3 * i + k], axis, -k))

    def index_rows():
        lane = lax.broadcasted_iota(jnp.int32, (1, 128), 1)
        h = lax.rem(me[2] - lax.rem(lane, 8) + 8, 8)
        key = LOCAL + group_rank(h) * 32 + (lane // 32) * 8 + lax.rem(lane // 8, 4) * 2
        wanted = lists_v[0]
        there = rdst_v[...]
        near = jnp.concatenate([ldst_v[...], jnp.full((1, 64), -1, jnp.int32)], axis=1)
        rows = [there[0:1], there[1:2]]
        given = [jnp.where(wanted[c : c + 1] >= 0, rows[c], -1) for c in range(2)] + [near]
        keys = [key, key + 1, lane]
        none = jnp.zeros((4, 128), jnp.int32)
        ask = jnp.concatenate(rows + [near, lane, none], axis=0).T
        limit = jnp.concatenate(
            keys + [jnp.full((1, 128), TILES, jnp.int32), none], axis=0
        ).T
        found = jnp.full((128, 128), -1, jnp.int32)
        column_of = lax.broadcasted_iota(jnp.int32, (128, 128), 1)
        for r in range(4):
            best = jnp.full((128, 128), -1, jnp.int32)
            for c in range(3):
                match = (ask[:, r : r + 1] == given[c]) & (keys[c] < limit[:, r : r + 1])
                best = jnp.maximum(best, jnp.where(match, keys[c], -1))
            top = jnp.max(best, axis=1, keepdims=True)
            found = jnp.where(column_of == r, top, found)
        found = jnp.where(found < 0, TILES, found)
        rows_v[...] = found.T[0:8]

    def lists_end():
        local(rows_v, rows_s).wait()
        for copy in list_in:
            copy.wait_recv()
        local(lists_v, lists_s).wait()

    def half_forward_first(t, d):
        here = d % 4
        part_of = pl.ds(0 if d == 1 else 4, 4)
        ring = sets[t][0]
        mid_in[t, d].wait_recv()
        far_in[t, d] = remote(ring.at[here, part_of], ring.at[2, part_of], KINDS[t][0], d)

    def first_end(t):
        for d in (1, -1):
            copy = far_in.pop((t, d), None)
            if copy is not None:
                copy.wait_recv()

    def z_arrival(t, h):
        z_in[t, h].wait_recv()
        d = 1 if h > 0 else -1
        limit = reach[t][0] if h > 0 else reach[t][1]
        here = sets[t][0].at[h % 8]
        if abs(h) < limit:
            z_in[t, h + d] = remote(here, sets[t][0].at[(h + d) % 8], Z, d)
        for e in (1, -1):
            mid_in[t, e, h] = remote(here, sets[t][e % 4].at[h % 8], KINDS[t][1], e)

    def half_forward(t, e, h):
        q = h % 8
        half = pl.ds(0 if e == 1 else 4, 4)
        mid_in[t, e, h].wait_recv()
        far_in[t, e, h] = remote(
            sets[t][e % 4].at[q, half], sets[t][2].at[q, half], KINDS[t][1], e
        )

    def half_end(t):
        for h in (0, 1, -1, 2, -2, 3, -3, (-4, 4)[t]):
            for e in (1, -1):
                far_in[t, e, h].wait_recv()

    def wide_start(t, q):
        if q == 2:
            first_end(t)
        source = own(t) if q == 0 else sets[t][0].at[q]
        for d in (1, -1):
            wide_in[t, d, q] = remote(source, sets[t][d % 8].at[q], Z, d)

    def wide_arrival(t, h, q):
        wide_in[t, h, q].wait_recv()
        d = 1 if h > 0 else -1
        limit = reach[t][0] if h > 0 else reach[t][1]
        if abs(h) < limit:
            wide_in[t, h + d, q] = remote(
                sets[t][h % 8].at[q], sets[t][(h + d) % 8].at[q], Z, d
            )

    def pack(t, g):
        a, b, c = KINDS[t]
        if t > 1 and g == 0:
            first_end(t)
        if t < 2 and g == 2:
            half_end(t)
        n = SIZES[a]
        source = sets[t][g]
        target = packs[t]
        fixed = lax.rem(me[b] - g + SIZES[b], SIZES[b])
        rows = pl.ds(SLICE * t, SLICE)

        def spot(there, *rest):
            where = [None, None, None]
            where[c] = me[c]
            where[b] = fixed
            where[a] = there
            return (where[0], where[1], where[2]) + rest

        def one(j, carry):
            there = lax.rem(me[a] - j + n, n)
            owner = me[c] * STRIDES[c] + fixed * STRIDES[b] + there * STRIDES[a]
            for k in range(4):
                slot = 0 if k == 0 else (k if c == X else 3 + k)
                for s in range(2):
                    index = jnp.clip(lists_s[slot, s, owner], 0, NB - 1)
                    value = source[j, index]
                    if k == 0:
                        pulled[spot(there, s, rows, slice(None))] = value
                    else:
                        target[k - 1, g, there, s] = value
            return carry

        lax.fori_loop(0, n, one, 0)
        to = pulled.at[spot(slice(None), slice(None), rows, slice(None))]
        last_in[t, g] = [remote(target.at[k - 1, g], to, c, k) for k in (1, 3, 2)]

    def arrived(t, g):
        for copy in last_in[t, g]:
            copy.wait_recv()

    def local_tiles(start, stop):
        if start == 0:
            load_lt.wait()

        def eight(i, carry):
            values = []
            for j in range(8):
                k = i * 8 + j
                values.append(
                    jnp.dot(
                        lt[k], hist[lsrc_s[0, k]], preferred_element_type=jnp.float32
                    )
                )
            for j in range(8):
                k = i * 8 + j
                sums[k] = sums[rows_s[2, k]] + values[j]
            return carry

        lax.fori_loop(start, stop, eight, 0)

    def remote_tiles(n):
        g = order[n]
        first = LOCAL + 32 * n
        tiles = rt.at[n % SLOTS]
        z = lax.rem(me[2] - g + 8, 8)

        def eight(i, carry):
            values = []
            for j in range(4):
                for c in range(2):
                    values.append(
                        jnp.dot(
                            tiles[i, j, c], pulled[i, j, z, c], preferred_element_type=jnp.float32
                        )
                    )
            for j in range(4):
                o = i * 32 + j * 8 + z
                for c in range(2):
                    sums[first + i * 8 + j * 2 + c] = (
                        sums[rows_s[c, o]] + values[2 * j + c]
                    )
            return carry

        lax.fori_loop(0, 4, eight, 0)


    z_start(0)
    z_start(1)
    first_start(2)
    first_start(3)
    mid_start(0)
    mid_start(1)
    lists_start()
    for t in range(4):
        sets[t][0][0] = hist[:, SLICE * t : SLICE * (t + 1), :]
    index_rows()
    steps = {
        "z": z_arrival,
        "m": half_forward,
        "f": half_forward_first,
        "s": wide_start,
        "w": wide_arrival,
        "p": pack,
    }
    packed = 0
    for event in EVENTS:
        if event[0] == "p":
            if packed == 0:
                lists_end()
            packed += 1
        steps[event[0]](*event[1:])
        if event[0] == "p" and packed > 10 and packed <= 18:
            local_tiles(packed - 11, packed - 10)
    for t in (0, 1):
        for g in (0, 1, 3, 2):
            arrived(t, g)
    for n, g in enumerate(order):
        arrived(2, g)
        arrived(3, g)
        tiles_in[n].wait()
        remote_tiles(n)
        if n + SLOTS < 8:
            tiles_in.append(load_tiles(n + SLOTS))
    load_cot.wait()
    load_weight.wait()
    load_bias.wait()
    shifts = []
    for t in range(NB):
        following[t] = sums[rows_s[3, NB + t]].astype(jnp.bfloat16)
        shifts.append(send(following.at[t], coming.at[t], up, f))
    swaps = []
    w_mine = weight[pl.ds(pl.multiple_of(f * HALF, HALF), HALF), :]
    w_other = weight[pl.ds(pl.multiple_of((1 - f) * HALF, HALF), HALF), :]
    b = bias[...]
    g_mine = jnp.zeros((HALF, HALF), jnp.float32)
    g_other = jnp.zeros((HALF, HALF), jnp.float32)
    g_bias = jnp.zeros((8, HALF), jnp.float32)
    for u in range(NB + LAG):
        if u < NB:
            mine = sums[rows_s[3, u]]
            shifts[u].wait_recv()
            agg[u] = (mine + coming[u].astype(jnp.float32)).astype(jnp.bfloat16)
            swaps.append(send(agg.at[u], other.at[u], p, 1 - f))
        t = u - LAG
        if t < 0:
            continue
        swaps[t].wait_recv()
        a0 = agg[t]
        a1 = other[t]
        v = (
            jnp.dot(a0, w_mine, preferred_element_type=jnp.float32)
            + jnp.dot(a1, w_other, preferred_element_type=jnp.float32)
            + b
        )
        v2 = v * v
        th = jnp.tanh(ROOT * (v + CUBIC * (v2 * v)))
        half = 0.5 * (1.0 + th)
        rows = slice(BLK * t, BLK * (t + 1))
        new_rows[rows, :] = (v * half).astype(jnp.bfloat16)
        slope = half + (0.5 * ROOT) * v * (1.0 - th * th) * (1.0 + (3.0 * CUBIC) * v2)
        gp = (cot[rows, :].astype(jnp.float32) * slope).astype(jnp.bfloat16)
        dims = (((0,), (0,)), ((), ()))
        g_mine += lax.dot_general(a0, gp, dims, preferred_element_type=jnp.float32)
        g_other += lax.dot_general(a1, gp, dims, preferred_element_type=jnp.float32)
        g_bias += jnp.sum(gp.astype(jnp.float32).reshape(16, 8, HALF), axis=0)
    terms[pl.ds(f * 8, 8), 0:16, :] = g_mine.reshape(8, 16, HALF)
    terms[pl.ds((1 - f) * 8, 8), 0:16, :] = g_other.reshape(8, 16, HALF)
    terms[:, 16:24, :] = jnp.zeros((16, 8, HALF), jnp.float32)
    terms[0, 16:24, :] = g_bias

    spot = me[0] * 4 + me[1]
    ins = [send(terms.at[d // 8], part.at[i], d, f) for i, d in enumerate(flat)]
    total = terms[spot]
    for i in range(15):
        ins[i].wait_recv()
        total = total + part[i]
    column_sums[me[2]] = total
    ins = [send(column_sums.at[me[2]], column_sums.at[me[2]], d, f) for d in column]
    for copy in ins:
        copy.wait_recv()
    total = column_sums[0]
    for k in range(1, 8):
        total = total + column_sums[k]
    final[spot] = total
    ins = [send(final.at[spot], final.at[spot], d, f) for d in flat]
    for copy in ins:
        copy.wait_recv()
    for k in range(16):
        grad_weight[16 * k : 16 * (k + 1), :] = final[k, 0:16, :]
    grad_bias[...] = jnp.sum(final[0, 16:24, :], axis=0, keepdims=True)
    for copy in remote_copies:
        copy.wait_send()


def step(*arrays):
    vm = pl.BlockSpec(memory_space=pltpu.VMEM)
    hbm = pl.BlockSpec(memory_space=pl.ANY)
    bf16 = jnp.bfloat16
    f32 = jnp.float32
    return pl.pallas_call(
        step_kernel,
        out_shape=(
            jax.ShapeDtypeStruct((NB * BLK, HALF), bf16),
            jax.ShapeDtypeStruct((2 * HALF, HALF), f32),
            jax.ShapeDtypeStruct((1, HALF), f32),
        ),
        in_specs=[hbm] * 10,
        out_specs=(vm, vm, vm),
        scratch_shapes=[pltpu.VMEM((8, NB, SLICE, HALF), bf16)] * 8
        + [pltpu.VMEM((4, NB, SLICE, HALF), bf16)] * 16
        + [pltpu.VMEM((3, 4, 8, 2, SLICE, HALF), bf16)] * 2
        + [pltpu.VMEM((3, 8, 4, 2, SLICE, HALF), bf16)] * 2
        + [
            pltpu.VMEM((7, 2, 128), jnp.int32),
            pltpu.SMEM((7, 2, 128), jnp.int32),
            pltpu.VMEM((2, 128), jnp.int32),
            pltpu.VMEM((1, 64), jnp.int32),
            pltpu.SMEM((1, 64), jnp.int32),
            pltpu.VMEM((8, 128), jnp.int32),
            pltpu.SMEM((8, 128), jnp.int32),
            pltpu.VMEM((2 * HALF, HALF), bf16),
            pltpu.VMEM((1, HALF), f32),
            pltpu.VMEM((NB, BLK, HALF), bf16),
            pltpu.VMEM((SLOTS, 4, 4, 2, BLK, BLK), bf16),
            pltpu.VMEM((LOCAL, BLK, BLK), bf16),
            pltpu.VMEM((NB * BLK, HALF), bf16),
            pltpu.VMEM((4, 4, 8, 2, BLK, HALF), bf16),
            pltpu.VMEM((TILES + 1, BLK, HALF), f32),
            pltpu.VMEM((NB, BLK, HALF), bf16),
            pltpu.VMEM((NB, BLK, HALF), bf16),
            pltpu.VMEM((NB, BLK, HALF), bf16),
            pltpu.VMEM((NB, BLK, HALF), bf16),
            pltpu.VMEM((16, PIECE, HALF), f32),
            pltpu.VMEM((15, PIECE, HALF), f32),
            pltpu.VMEM((8, PIECE, HALF), f32),
            pltpu.VMEM((16, PIECE, HALF), f32),
            pltpu.SemaphoreType.DMA((320,)),
            pltpu.SemaphoreType.DMA((320,)),
            pltpu.SemaphoreType.DMA((24,)),
        ],
        compiler_params=pltpu.CompilerParams(
            collective_id=0, has_side_effects=True, vmem_limit_bytes=51 << 20
        ),
        name="step",
    )(*arrays)


def per_device(
    history,
    pull_list,
    remote_tiles,
    remote_dst,
    local_tiles,
    local_src,
    local_dst,
    weight,
    bias,
    cotangent,
):
    new_rows, grad_weight, grad_bias = step(
        history.reshape(NB, BLK, HALF),
        pull_list[0].T,
        remote_dst[0].T,
        local_src,
        local_dst,
        remote_tiles[0].reshape(4, 4, 8, 2, BLK, BLK),
        local_tiles,
        cotangent,
        weight,
        bias.reshape(1, HALF),
    )
    return new_rows, grad_weight, grad_bias.reshape(HALF)


def solution(mesh):
    placed = (
        P("dom", "feat"),
        P("dom", None, None),
        P("dom", None, None, None, None),
        P("dom", None, None),
        P("dom", None, None),
        P("dom", None),
        P("dom", None),
        P(None, "feat"),
        P("feat"),
        P("dom", "feat"),
    )
    return jax.shard_map(
        per_device,
        mesh=mesh,
        in_specs=placed,
        out_specs=(P("dom", "feat"), P(None, "feat"), P("feat")),
        check_vma=False,
    )
```

```python
import functools

import jax
import jax.numpy as jnp
from jax import lax
from jax.sharding import PartitionSpec as P
from jax.experimental import pallas as pl
from jax.experimental.pallas import tpu as pltpu

MESH = pl.DeviceIdType.MESH
X, Y, Z = 0, 1, 2
SIZES = (4, 4, 8)
STRIDES = (32, 8, 1)
NB = 8
BLK = 128
HALF = 128
SLICE = 32
KINDS = ((Z, Y, X), (Z, X, Y), (Y, Z, X), (X, Z, Y))


def coords():
    p = lax.axis_index("dom")
    return (p // 32, lax.rem(p // 8, 4), lax.rem(p, 8)), lax.axis_index("feat")


def group_rank(h):
    return jnp.where(h == 0, 0, jnp.where(h <= 4, 2 * h - 1, 2 * (8 - h)))


def moved(me, axis, offset):
    n = SIZES[axis]
    there = list(me)
    there[axis] = lax.rem(me[axis] + (offset % n), n)
    return there[0] * 32 + there[1] * 8 + there[2]


PIECE = 24
ROOT = 0.7978845608028654
CUBIC = 0.044715
TILES = 320
LOCAL = 64
LAG = 2
SLOTS = 3
EVENTS = (
    ("s", 2, 0), ("z", 0, 1), ("z", 0, -1), ("f", 2, 1), ("f", 2, -1), ("f", 3, 1), ("f", 3, -1),
    ("z", 1, 1), ("z", 1, -1), ("m", 0, 1, 0), ("m", 0, -1, 0), ("m", 1, 1, 0), ("m", 1, -1, 0),
    ("w", 2, 1, 0), ("w", 2, -1, 0), ("m", 0, 1, 1), ("m", 0, -1, 1), ("m", 1, 1, 1), ("m", 1, -1, 1),
    ("p", 3, 0), ("z", 0, 2), ("z", 0, -2), ("m", 0, 1, -1), ("m", 0, -1, -1), ("p", 2, 0), ("m", 1, 1, -1),
    ("m", 1, -1, -1), ("z", 1, 2), ("z", 1, -2), ("w", 2, 2, 0), ("w", 2, -2, 0), ("z", 0, 3), ("z", 0, -3),
    ("s", 3, 0), ("z", 1, 3), ("z", 1, -3), ("m", 0, 1, 2), ("m", 0, -1, 2), ("w", 2, 3, 0), ("w", 2, -3, 0),
    ("s", 2, 1), ("m", 1, 1, 2), ("m", 1, -1, 2), ("m", 0, 1, -2), ("m", 0, -1, -2), ("w", 3, 1, 0),
    ("z", 0, -4), ("s", 2, 3), ("m", 1, 1, -2), ("m", 1, -1, -2), ("z", 1, 4), ("w", 3, -1, 0),
    ("m", 0, 1, 3), ("m", 0, -1, 3), ("m", 1, 1, 3), ("m", 1, -1, 3), ("w", 2, 4, 0), ("w", 2, -1, 1),
    ("m", 0, 1, -3), ("m", 0, -1, -3), ("m", 1, 1, -3), ("m", 1, -1, -3), ("w", 2, 1, 1), ("w", 2, -1, 3),
    ("p", 1, 0), ("p", 0, 0), ("w", 3, 2, 0), ("w", 3, -2, 0), ("m", 0, 1, -4), ("m", 0, -1, -4),
    ("m", 1, 1, 4), ("m", 1, -1, 4), ("w", 2, 1, 3), ("w", 2, -2, 1), ("w", 2, 2, 1), ("w", 2, -2, 3),
    ("w", 3, 3, 0), ("w", 3, -3, 0), ("s", 3, 1), ("p", 1, 1), ("w", 2, 2, 3), ("w", 2, -3, 1), ("p", 0, 1),
    ("w", 2, 3, 1), ("w", 2, -3, 3), ("s", 3, 3), ("w", 3, 1, 1), ("w", 3, -4, 0), ("s", 3, 2),
    ("w", 2, 3, 3), ("w", 3, -1, 1), ("p", 1, 3), ("p", 0, 3), ("s", 2, 2), ("w", 2, 4, 1), ("w", 3, -1, 3),
    ("w", 3, 1, 3), ("w", 3, -1, 2), ("w", 3, 2, 1), ("w", 3, -2, 1), ("w", 3, 1, 2), ("w", 2, -1, 2),
    ("p", 1, 2), ("p", 0, 2), ("w", 2, 4, 3), ("w", 3, -2, 3), ("w", 2, 1, 2), ("w", 3, -2, 2),
    ("w", 3, 2, 3), ("w", 3, -3, 1), ("w", 3, 3, 1), ("w", 2, -2, 2), ("p", 3, 7), ("w", 3, 2, 2),
    ("w", 3, -3, 3), ("p", 2, 7), ("w", 2, 2, 2), ("w", 3, -3, 2), ("p", 3, 1), ("w", 3, 3, 3),
    ("w", 3, -4, 1), ("p", 2, 1), ("w", 3, 3, 2), ("w", 2, -3, 2), ("p", 3, 6), ("w", 2, 3, 2),
    ("w", 3, -4, 3), ("p", 2, 6), ("w", 3, -4, 2), ("p", 3, 2), ("w", 2, 4, 2), ("p", 2, 2), ("p", 3, 5),
    ("p", 2, 5), ("p", 3, 3), ("p", 2, 3), ("p", 3, 4), ("p", 2, 4),
)


def step_kernel(
    history,
    plist,
    rdst,
    lsrc,
    ldst,
    rtiles,
    ltiles,
    cotangent,
    weight_hbm,
    bias_hbm,
    new_rows,
    grad_weight,
    grad_bias,
    *scratch,
):
    sets = [scratch[0:4], scratch[4:8], scratch[8:16], scratch[16:24]]
    packs = scratch[24:28]
    (
        lists_v,
        lists_s,
        rdst_v,
        ldst_v,
        lsrc_s,
        rows_v,
        rows_s,
        weight,
        bias,
        hist,
        rt,
        lt,
        cot,
        pulled,
        sums,
        following,
        coming,
        agg,
        other,
        terms,
        part,
        column_sums,
        final,
        send_sems,
        recv_sems,
        local_sems,
    ) = scratch[28:]
    me, f = coords()
    p = lax.axis_index("dom")
    used = [0, 0]
    remote_copies = []

    def send(src, dst, dom, feat):
        i = used[0]
        used[0] += 1
        copy = pltpu.make_async_remote_copy(
            src_ref=src,
            dst_ref=dst,
            send_sem=send_sems.at[i],
            recv_sem=recv_sems.at[i],
            device_id=(dom, feat),
            device_id_type=MESH,
        )
        copy.start()
        remote_copies.append(copy)
        return copy

    def remote(src, dst, axis, offset):
        return send(src, dst, moved(me, axis, offset), f)

    def local(src, dst):
        i = used[1]
        used[1] += 1
        copy = pltpu.make_async_copy(src, dst, local_sems.at[i])
        copy.start()
        return copy

    def own(t):
        return hist.at[:, pl.ds(SLICE * t, SLICE), :]

    load_hist = local(history, hist)
    small = [
        local(plist, lists_v.at[0]),
        local(rdst, rdst_v),
        local(ldst, ldst_v),
        local(lsrc, lsrc_s),
    ]
    up = lax.rem(p + 1, 128)
    column = [moved(me, Z, k) for k in range(1, 8)]
    flat = [
        lax.rem(me[0] + i, 4) * 32 + lax.rem(me[1] + j, 4) * 8 + me[2]
        for i in range(4)
        for j in range(4)
        if i or j
    ]
    barrier = pltpu.get_barrier_semaphore()
    near = ((X, 1), (X, 2), (X, 3), (Y, 1), (Y, 2), (Y, 3), (Z, 1), (Z, 7))
    greeted = [(p, 1 - f)] + [(moved(me, axis, k), f) for axis, k in near]
    for d in greeted:
        pl.semaphore_signal(barrier, inc=1, device_id=d, device_id_type=MESH)
    order = (0, 1, 7, 2, 6, 3, 5, 4)

    def load_tiles(i):
        z = lax.rem(me[2] - order[i] + 8, 8)
        return local(rtiles.at[:, :, z], rt.at[i % SLOTS])

    tiles_in = [load_tiles(i) for i in range(SLOTS)]
    load_lt = local(ltiles, lt)
    load_cot = local(cotangent, cot)
    load_weight = local(weight_hbm, weight)
    load_bias = local(bias_hbm, bias)
    sums[TILES] = jnp.zeros((BLK, HALF), jnp.float32)
    load_hist.wait()
    for copy in small:
        copy.wait()
    pl.semaphore_wait(barrier, len(greeted))

    z_in = {}
    mid_in = {}
    wide_in = {}
    far_in = {}
    last_in = {}
    list_in = []
    reach = {0: (3, 4), 1: (4, 3), 2: (4, 3), 3: (3, 4)}

    def z_start(t):
        for d in (1, -1):
            z_in[t, d] = remote(own(t), sets[t][0].at[d % 8], Z, d)

    def first_start(t):
        for d in (1, -1):
            mid_in[t, d] = remote(own(t), sets[t][0].at[d % 4], KINDS[t][0], d)

    def mid_start(t):
        for d in (1, -1):
            mid_in[t, d, 0] = remote(own(t), sets[t][d % 4].at[0], KINDS[t][1], d)

    def lists_start():
        for i, axis in enumerate((X, Y)):
            for k in (1, 2, 3):
                list_in.append(remote(lists_v.at[0], lists_v.at[3 * i + k], axis, -k))

    def index_rows():
        lane = lax.broadcasted_iota(jnp.int32, (1, 128), 1)
        h = lax.rem(me[2] - lax.rem(lane, 8) + 8, 8)
        key = LOCAL + group_rank(h) * 32 + (lane // 32) * 8 + lax.rem(lane // 8, 4) * 2
        wanted = lists_v[0]
        there = rdst_v[...]
        near = jnp.concatenate([ldst_v[...], jnp.full((1, 64), -1, jnp.int32)], axis=1)
        rows = [there[0:1], there[1:2]]
        given = [jnp.where(wanted[c : c + 1] >= 0, rows[c], -1) for c in range(2)] + [near]
        keys = [key, key + 1, lane]
        none = jnp.zeros((4, 128), jnp.int32)
        ask = jnp.concatenate(rows + [near, lane, none], axis=0).T
        limit = jnp.concatenate(
            keys + [jnp.full((1, 128), TILES, jnp.int32), none], axis=0
        ).T
        found = jnp.full((128, 128), -1, jnp.int32)
        column_of = lax.broadcasted_iota(jnp.int32, (128, 128), 1)
        for r in range(4):
            best = jnp.full((128, 128), -1, jnp.int32)
            for c in range(3):
                match = (ask[:, r : r + 1] == given[c]) & (keys[c] < limit[:, r : r + 1])
                best = jnp.maximum(best, jnp.where(match, keys[c], -1))
            top = jnp.max(best, axis=1, keepdims=True)
            found = jnp.where(column_of == r, top, found)
        found = jnp.where(found < 0, TILES, found)
        rows_v[...] = found.T[0:8]

    def lists_end():
        local(rows_v, rows_s).wait()
        for copy in list_in:
            copy.wait_recv()
        local(lists_v, lists_s).wait()

    def half_forward_first(t, d):
        here = d % 4
        part_of = pl.ds(0 if d == 1 else 4, 4)
        ring = sets[t][0]
        mid_in[t, d].wait_recv()
        far_in[t, d] = remote(ring.at[here, part_of], ring.at[2, part_of], KINDS[t][0], d)

    def first_end(t):
        for d in (1, -1):
            copy = far_in.pop((t, d), None)
            if copy is not None:
                copy.wait_recv()

    def z_arrival(t, h):
        z_in[t, h].wait_recv()
        d = 1 if h > 0 else -1
        limit = reach[t][0] if h > 0 else reach[t][1]
        here = sets[t][0].at[h % 8]
        if abs(h) < limit:
            z_in[t, h + d] = remote(here, sets[t][0].at[(h + d) % 8], Z, d)
        for e in (1, -1):
            mid_in[t, e, h] = remote(here, sets[t][e % 4].at[h % 8], KINDS[t][1], e)

    def half_forward(t, e, h):
        q = h % 8
        half = pl.ds(0 if e == 1 else 4, 4)
        mid_in[t, e, h].wait_recv()
        far_in[t, e, h] = remote(
            sets[t][e % 4].at[q, half], sets[t][2].at[q, half], KINDS[t][1], e
        )

    def half_end(t):
        for h in (0, 1, -1, 2, -2, 3, -3, (-4, 4)[t]):
            for e in (1, -1):
                far_in[t, e, h].wait_recv()

    def wide_start(t, q):
        if q == 2:
            first_end(t)
        source = own(t) if q == 0 else sets[t][0].at[q]
        for d in (1, -1):
            wide_in[t, d, q] = remote(source, sets[t][d % 8].at[q], Z, d)

    def wide_arrival(t, h, q):
        wide_in[t, h, q].wait_recv()
        d = 1 if h > 0 else -1
        limit = reach[t][0] if h > 0 else reach[t][1]
        if abs(h) < limit:
            wide_in[t, h + d, q] = remote(
                sets[t][h % 8].at[q], sets[t][(h + d) % 8].at[q], Z, d
            )

    def pack(t, g):
        a, b, c = KINDS[t]
        if t > 1 and g == 0:
            first_end(t)
        if t < 2 and g == 2:
            half_end(t)
        n = SIZES[a]
        source = sets[t][g]
        target = packs[t]
        fixed = lax.rem(me[b] - g + SIZES[b], SIZES[b])
        rows = pl.ds(SLICE * t, SLICE)

        def spot(there, *rest):
            where = [None, None, None]
            where[c] = me[c]
            where[b] = fixed
            where[a] = there
            return (where[0], where[1], where[2]) + rest

        def one(j, carry):
            there = lax.rem(me[a] - j + n, n)
            owner = me[c] * STRIDES[c] + fixed * STRIDES[b] + there * STRIDES[a]
            for k in range(4):
                slot = 0 if k == 0 else (k if c == X else 3 + k)
                for s in range(2):
                    index = jnp.clip(lists_s[slot, s, owner], 0, NB - 1)
                    value = source[j, index]
                    if k == 0:
                        pulled[spot(there, s, rows, slice(None))] = value
                    else:
                        target[k - 1, g, there, s] = value
            return carry

        lax.fori_loop(0, n, one, 0)
        to = pulled.at[spot(slice(None), slice(None), rows, slice(None))]
        last_in[t, g] = [remote(target.at[k - 1, g], to, c, k) for k in (1, 3, 2)]

    def arrived(t, g):
        for copy in last_in[t, g]:
            copy.wait_recv()

    def local_tiles(start, stop):
        if start == 0:
            load_lt.wait()

        def eight(i, carry):
            values = []
            for j in range(8):
                k = i * 8 + j
                values.append(
                    jnp.dot(
                        lt[k], hist[lsrc_s[0, k]], preferred_element_type=jnp.float32
                    )
                )
            for j in range(8):
                k = i * 8 + j
                sums[k] = sums[rows_s[2, k]] + values[j]
            return carry

        lax.fori_loop(start, stop, eight, 0)

    def remote_tiles(n):
        g = order[n]
        first = LOCAL + 32 * n
        tiles = rt.at[n % SLOTS]
        z = lax.rem(me[2] - g + 8, 8)

        def eight(i, carry):
            values = []
            for j in range(4):
                for c in range(2):
                    values.append(
                        jnp.dot(
                            tiles[i, j, c], pulled[i, j, z, c], preferred_element_type=jnp.float32
                        )
                    )
            for j in range(4):
                o = i * 32 + j * 8 + z
                for c in range(2):
                    sums[first + i * 8 + j * 2 + c] = (
                        sums[rows_s[c, o]] + values[2 * j + c]
                    )
            return carry

        lax.fori_loop(0, 4, eight, 0)


    z_start(0)
    z_start(1)
    first_start(2)
    first_start(3)
    mid_start(0)
    mid_start(1)
    lists_start()
    for t in range(4):
        sets[t][0][0] = hist[:, SLICE * t : SLICE * (t + 1), :]
    index_rows()
    steps = {
        "z": z_arrival,
        "m": half_forward,
        "f": half_forward_first,
        "s": wide_start,
        "w": wide_arrival,
        "p": pack,
    }
    packed = 0
    for event in EVENTS:
        if event[0] == "p":
            if packed == 0:
                lists_end()
            packed += 1
        steps[event[0]](*event[1:])
        if event[0] == "p" and packed > 10 and packed <= 18:
            local_tiles(packed - 11, packed - 10)
    for t in (0, 1):
        for g in (0, 1, 3, 2):
            arrived(t, g)
    for n, g in enumerate(order):
        arrived(2, g)
        arrived(3, g)
        tiles_in[n].wait()
        remote_tiles(n)
        if n + SLOTS < 8:
            tiles_in.append(load_tiles(n + SLOTS))
    load_cot.wait()
    load_weight.wait()
    load_bias.wait()
    shifts = []
    for t in range(NB):
        following[t] = sums[rows_s[3, NB + t]].astype(jnp.bfloat16)
        shifts.append(send(following.at[t], coming.at[t], up, f))
    swaps = []
    w_mine = weight[pl.ds(pl.multiple_of(f * HALF, HALF), HALF), :]
    w_other = weight[pl.ds(pl.multiple_of((1 - f) * HALF, HALF), HALF), :]
    b = bias[...]
    g_mine = jnp.zeros((HALF, HALF), jnp.float32)
    g_other = jnp.zeros((HALF, HALF), jnp.float32)
    g_bias = jnp.zeros((8, HALF), jnp.float32)
    for u in range(NB + LAG):
        if u < NB:
            mine = sums[rows_s[3, u]]
            shifts[u].wait_recv()
            agg[u] = (mine + coming[u].astype(jnp.float32)).astype(jnp.bfloat16)
            swaps.append(send(agg.at[u], other.at[u], p, 1 - f))
        t = u - LAG
        if t < 0:
            continue
        swaps[t].wait_recv()
        a0 = agg[t]
        a1 = other[t]
        v = (
            jnp.dot(a0, w_mine, preferred_element_type=jnp.float32)
            + jnp.dot(a1, w_other, preferred_element_type=jnp.float32)
            + b
        )
        v2 = v * v
        th = jnp.tanh(ROOT * (v + CUBIC * (v2 * v)))
        half = 0.5 * (1.0 + th)
        rows = slice(BLK * t, BLK * (t + 1))
        new_rows[rows, :] = (v * half).astype(jnp.bfloat16)
        slope = half + (0.5 * ROOT) * v * (1.0 - th * th) * (1.0 + (3.0 * CUBIC) * v2)
        gp = (cot[rows, :].astype(jnp.float32) * slope).astype(jnp.bfloat16)
        dims = (((0,), (0,)), ((), ()))
        g_mine += lax.dot_general(a0, gp, dims, preferred_element_type=jnp.float32)
        g_other += lax.dot_general(a1, gp, dims, preferred_element_type=jnp.float32)
        g_bias += jnp.sum(gp.astype(jnp.float32).reshape(16, 8, HALF), axis=0)
    terms[pl.ds(f * 8, 8), 0:16, :] = g_mine.reshape(8, 16, HALF)
    terms[pl.ds((1 - f) * 8, 8), 0:16, :] = g_other.reshape(8, 16, HALF)
    terms[:, 16:24, :] = jnp.zeros((16, 8, HALF), jnp.float32)
    terms[0, 16:24, :] = g_bias

    spot = me[0] * 4 + me[1]
    ins = [send(terms.at[d // 8], part.at[i], d, f) for i, d in enumerate(flat)]
    total = terms[spot]
    for i in range(15):
        ins[i].wait_recv()
        total = total + part[i]
    column_sums[me[2]] = total
    ins = [send(column_sums.at[me[2]], column_sums.at[me[2]], d, f) for d in column]
    for copy in ins:
        copy.wait_recv()
    total = column_sums[0]
    for k in range(1, 8):
        total = total + column_sums[k]
    final[spot] = total
    ins = [send(final.at[spot], final.at[spot], d, f) for d in flat]
    for copy in ins:
        copy.wait_recv()
    for k in range(16):
        grad_weight[16 * k : 16 * (k + 1), :] = final[k, 0:16, :]
    grad_bias[...] = jnp.sum(final[0, 16:24, :], axis=0, keepdims=True)
    for copy in remote_copies:
        copy.wait_send()


def step(*arrays):
    vm = pl.BlockSpec(memory_space=pltpu.VMEM)
    hbm = pl.BlockSpec(memory_space=pltpu.HBM)
    bf16 = jnp.bfloat16
    f32 = jnp.float32
    return pl.pallas_call(
        step_kernel,
        out_shape=(
            jax.ShapeDtypeStruct((NB * BLK, HALF), bf16),
            jax.ShapeDtypeStruct((2 * HALF, HALF), f32),
            jax.ShapeDtypeStruct((1, HALF), f32),
        ),
        in_specs=[hbm] * 10,
        out_specs=(vm, vm, vm),
        scratch_shapes=[pltpu.VMEM((8, NB, SLICE, HALF), bf16)] * 8
        + [pltpu.VMEM((4, NB, SLICE, HALF), bf16)] * 16
        + [pltpu.VMEM((3, 4, 8, 2, SLICE, HALF), bf16)] * 2
        + [pltpu.VMEM((3, 8, 4, 2, SLICE, HALF), bf16)] * 2
        + [
            pltpu.VMEM((7, 2, 128), jnp.int32),
            pltpu.SMEM((7, 2, 128), jnp.int32),
            pltpu.VMEM((2, 128), jnp.int32),
            pltpu.VMEM((1, 64), jnp.int32),
            pltpu.SMEM((1, 64), jnp.int32),
            pltpu.VMEM((8, 128), jnp.int32),
            pltpu.SMEM((8, 128), jnp.int32),
            pltpu.VMEM((2 * HALF, HALF), bf16),
            pltpu.VMEM((1, HALF), f32),
            pltpu.VMEM((NB, BLK, HALF), bf16),
            pltpu.VMEM((SLOTS, 4, 4, 2, BLK, BLK), bf16),
            pltpu.VMEM((LOCAL, BLK, BLK), bf16),
            pltpu.VMEM((NB * BLK, HALF), bf16),
            pltpu.VMEM((4, 4, 8, 2, BLK, HALF), bf16),
            pltpu.VMEM((TILES + 1, BLK, HALF), f32),
            pltpu.VMEM((NB, BLK, HALF), bf16),
            pltpu.VMEM((NB, BLK, HALF), bf16),
            pltpu.VMEM((NB, BLK, HALF), bf16),
            pltpu.VMEM((NB, BLK, HALF), bf16),
            pltpu.VMEM((16, PIECE, HALF), f32),
            pltpu.VMEM((15, PIECE, HALF), f32),
            pltpu.VMEM((8, PIECE, HALF), f32),
            pltpu.VMEM((16, PIECE, HALF), f32),
            pltpu.SemaphoreType.DMA((320,)),
            pltpu.SemaphoreType.DMA((320,)),
            pltpu.SemaphoreType.DMA((24,)),
        ],
        compiler_params=pltpu.CompilerParams(
            collective_id=0, has_side_effects=True, vmem_limit_bytes=51 << 20
        ),
        name="step",
    )(*[pltpu.with_memory_space_constraint(a, pltpu.HBM) for a in arrays])


def per_device(
    history,
    pull_list,
    remote_tiles,
    remote_dst,
    local_tiles,
    local_src,
    local_dst,
    weight,
    bias,
    cotangent,
):
    new_rows, grad_weight, grad_bias = step(
        history.reshape(NB, BLK, HALF),
        pull_list[0].T,
        remote_dst[0].T,
        local_src,
        local_dst,
        remote_tiles[0].reshape(4, 4, 8, 2, BLK, BLK),
        local_tiles,
        cotangent,
        weight,
        bias.reshape(1, HALF),
    )
    return new_rows, grad_weight, grad_bias.reshape(HALF)


def solution(mesh):
    placed = (
        P("dom", "feat"),
        P("dom", None, None),
        P("dom", None, None, None, None),
        P("dom", None, None),
        P("dom", None, None),
        P("dom", None),
        P("dom", None),
        P(None, "feat"),
        P("feat"),
        P("dom", "feat"),
    )
    return jax.shard_map(
        per_device,
        mesh=mesh,
        in_specs=placed,
        out_specs=(P("dom", "feat"), P(None, "feat"), P("feat")),
        check_vma=False,
    )
```

```python
import functools

import jax
import jax.numpy as jnp
from jax import lax
from jax.sharding import PartitionSpec as P
from jax.experimental import pallas as pl
from jax.experimental.pallas import tpu as pltpu

MESH = pl.DeviceIdType.MESH
X, Y, Z = 0, 1, 2
SIZES = (4, 4, 8)
STRIDES = (32, 8, 1)
NB = 8
BLK = 128
HALF = 128
SLICE = 32
KINDS = ((Z, Y, X), (Z, X, Y), (Y, Z, X), (X, Z, Y))


def coords():
    p = lax.axis_index("dom")
    return (p // 32, lax.rem(p // 8, 4), lax.rem(p, 8)), lax.axis_index("feat")


def group_rank(h):
    return jnp.where(h == 0, 0, jnp.where(h <= 4, 2 * h - 1, 2 * (8 - h)))


def moved(me, axis, offset):
    n = SIZES[axis]
    there = list(me)
    there[axis] = lax.rem(me[axis] + (offset % n), n)
    return there[0] * 32 + there[1] * 8 + there[2]


PIECE = 24
ROOT = 0.7978845608028654
CUBIC = 0.044715
TILES = 320
LOCAL = 64
LAG = 2
SLOTS = 3
EVENTS = (
    ("s", 2, 0), ("z", 0, 1), ("z", 0, -1), ("f", 2, 1), ("f", 2, -1), ("f", 3, 1), ("f", 3, -1),
    ("z", 1, 1), ("z", 1, -1), ("m", 0, 1, 0), ("m", 0, -1, 0), ("m", 1, 1, 0), ("m", 1, -1, 0),
    ("w", 2, 1, 0), ("w", 2, -1, 0), ("m", 0, 1, 1), ("m", 0, -1, 1), ("m", 1, 1, 1), ("m", 1, -1, 1),
    ("p", 3, 0), ("z", 0, 2), ("z", 0, -2), ("m", 0, 1, -1), ("m", 0, -1, -1), ("p", 2, 0), ("m", 1, 1, -1),
    ("m", 1, -1, -1), ("z", 1, 2), ("z", 1, -2), ("w", 2, 2, 0), ("w", 2, -2, 0), ("z", 0, 3), ("z", 0, -3),
    ("s", 3, 0), ("z", 1, 3), ("z", 1, -3), ("m", 0, 1, 2), ("m", 0, -1, 2), ("w", 2, 3, 0), ("w", 2, -3, 0),
    ("s", 2, 1), ("m", 1, 1, 2), ("m", 1, -1, 2), ("m", 0, 1, -2), ("m", 0, -1, -2), ("w", 3, 1, 0),
    ("z", 0, -4), ("s", 2, 3), ("m", 1, 1, -2), ("m", 1, -1, -2), ("z", 1, 4), ("w", 3, -1, 0),
    ("m", 0, 1, 3), ("m", 0, -1, 3), ("m", 1, 1, 3), ("m", 1, -1, 3), ("w", 2, 4, 0), ("w", 2, -1, 1),
    ("m", 0, 1, -3), ("m", 0, -1, -3), ("m", 1, 1, -3), ("m", 1, -1, -3), ("w", 2, 1, 1), ("w", 2, -1, 3),
    ("p", 1, 0), ("p", 0, 0), ("w", 3, 2, 0), ("w", 3, -2, 0), ("m", 0, 1, -4), ("m", 0, -1, -4),
    ("m", 1, 1, 4), ("m", 1, -1, 4), ("w", 2, 1, 3), ("w", 2, -2, 1), ("w", 2, 2, 1), ("w", 2, -2, 3),
    ("w", 3, 3, 0), ("w", 3, -3, 0), ("s", 3, 1), ("p", 1, 1), ("w", 2, 2, 3), ("w", 2, -3, 1), ("p", 0, 1),
    ("w", 2, 3, 1), ("w", 2, -3, 3), ("s", 3, 3), ("w", 3, 1, 1), ("w", 3, -4, 0), ("s", 3, 2),
    ("w", 2, 3, 3), ("w", 3, -1, 1), ("p", 1, 3), ("p", 0, 3), ("s", 2, 2), ("w", 2, 4, 1), ("w", 3, -1, 3),
    ("w", 3, 1, 3), ("w", 3, -1, 2), ("w", 3, 2, 1), ("w", 3, -2, 1), ("w", 3, 1, 2), ("w", 2, -1, 2),
    ("p", 1, 2), ("p", 0, 2), ("w", 2, 4, 3), ("w", 3, -2, 3), ("w", 2, 1, 2), ("w", 3, -2, 2),
    ("w", 3, 2, 3), ("w", 3, -3, 1), ("w", 3, 3, 1), ("w", 2, -2, 2), ("p", 3, 7), ("w", 3, 2, 2),
    ("w", 3, -3, 3), ("p", 2, 7), ("w", 2, 2, 2), ("w", 3, -3, 2), ("p", 3, 1), ("w", 3, 3, 3),
    ("w", 3, -4, 1), ("p", 2, 1), ("w", 3, 3, 2), ("w", 2, -3, 2), ("p", 3, 6), ("w", 2, 3, 2),
    ("w", 3, -4, 3), ("p", 2, 6), ("w", 3, -4, 2), ("p", 3, 2), ("w", 2, 4, 2), ("p", 2, 2), ("p", 3, 5),
    ("p", 2, 5), ("p", 3, 3), ("p", 2, 3), ("p", 3, 4), ("p", 2, 4),
)


def step_kernel(
    history,
    plist,
    rdst,
    lsrc,
    ldst,
    rtiles,
    ltiles,
    cotangent,
    weight_hbm,
    bias_hbm,
    new_rows,
    grad_weight,
    grad_bias,
    *scratch,
):
    sets = [scratch[0:4], scratch[4:8], scratch[8:16], scratch[16:24]]
    packs = scratch[24:28]
    (
        lists_v,
        lists_s,
        rdst_v,
        ldst_v,
        lsrc_s,
        rows_v,
        rows_s,
        weight,
        bias,
        hist,
        rt,
        lt,
        cot,
        pulled,
        sums,
        following,
        coming,
        agg,
        other,
        terms,
        part,
        column_sums,
        final,
        send_sems,
        recv_sems,
        local_sems,
    ) = scratch[28:]
    me, f = coords()
    p = lax.axis_index("dom")
    used = [0, 0]
    remote_copies = []

    def send(src, dst, dom, feat):
        i = used[0]
        used[0] += 1
        copy = pltpu.make_async_remote_copy(
            src_ref=src,
            dst_ref=dst,
            send_sem=send_sems.at[i],
            recv_sem=recv_sems.at[i],
            device_id=(dom, feat),
            device_id_type=MESH,
        )
        copy.start()
        remote_copies.append(copy)
        return copy

    def remote(src, dst, axis, offset):
        return send(src, dst, moved(me, axis, offset), f)

    def local(src, dst):
        i = used[1]
        used[1] += 1
        copy = pltpu.make_async_copy(src, dst, local_sems.at[i])
        copy.start()
        return copy

    def own(t):
        return hist.at[:, pl.ds(SLICE * t, SLICE), :]

    load_hist = local(history, hist)
    small = [
        local(plist, lists_v.at[0]),
        local(rdst, rdst_v),
        local(ldst, ldst_v),
        local(lsrc, lsrc_s),
    ]
    up = lax.rem(p + 1, 128)
    column = [moved(me, Z, k) for k in (4, 3, 5, 2, 6, 1, 7)]
    flat = [
        lax.rem(me[0] + i, 4) * 32 + lax.rem(me[1] + j, 4) * 8 + me[2]
        for i, j in (
            ((2, 2), (2, 1), (1, 2), (2, 3), (3, 2), (1, 1), (1, 3), (3, 1), (3, 3))
            + ((2, 0), (0, 2), (1, 0), (0, 1), (3, 0), (0, 3))
        )
    ]
    barrier = pltpu.get_barrier_semaphore()
    near = ((X, 1), (X, 2), (X, 3), (Y, 1), (Y, 2), (Y, 3), (Z, 1), (Z, 7))
    greeted = [(p, 1 - f)] + [(moved(me, axis, k), f) for axis, k in near]
    for d in greeted:
        pl.semaphore_signal(barrier, inc=1, device_id=d, device_id_type=MESH)
    order = (0, 1, 7, 2, 6, 3, 5, 4)

    def load_tiles(i):
        z = lax.rem(me[2] - order[i] + 8, 8)
        return local(rtiles.at[:, :, z], rt.at[i % SLOTS])

    tiles_in = [load_tiles(i) for i in range(SLOTS)]
    load_lt = local(ltiles, lt)
    load_cot = local(cotangent, cot)
    load_weight = local(weight_hbm, weight)
    load_bias = local(bias_hbm, bias)
    sums[TILES] = jnp.zeros((BLK, HALF), jnp.float32)
    load_hist.wait()
    for copy in small:
        copy.wait()
    pl.semaphore_wait(barrier, len(greeted))

    z_in = {}
    mid_in = {}
    wide_in = {}
    far_in = {}
    last_in = {}
    list_in = []
    reach = {0: (3, 4), 1: (4, 3), 2: (4, 3), 3: (3, 4)}

    def z_start(t):
        for d in (1, -1):
            z_in[t, d] = remote(own(t), sets[t][0].at[d % 8], Z, d)

    def first_start(t):
        for d in (1, -1):
            mid_in[t, d] = remote(own(t), sets[t][0].at[d % 4], KINDS[t][0], d)

    def mid_start(t):
        for d in (1, -1):
            mid_in[t, d, 0] = remote(own(t), sets[t][d % 4].at[0], KINDS[t][1], d)

    def lists_start():
        for i, axis in enumerate((X, Y)):
            for k in (1, 2, 3):
                list_in.append(remote(lists_v.at[0], lists_v.at[3 * i + k], axis, -k))

    def index_rows():
        lane = lax.broadcasted_iota(jnp.int32, (1, 128), 1)
        h = lax.rem(me[2] - lax.rem(lane, 8) + 8, 8)
        key = LOCAL + group_rank(h) * 32 + (lane // 32) * 8 + lax.rem(lane // 8, 4) * 2
        wanted = lists_v[0]
        there = rdst_v[...]
        near = jnp.concatenate([ldst_v[...], jnp.full((1, 64), -1, jnp.int32)], axis=1)
        rows = [there[0:1], there[1:2]]
        given = [jnp.where(wanted[c : c + 1] >= 0, rows[c], -1) for c in range(2)] + [near]
        keys = [key, key + 1, lane]
        none = jnp.zeros((4, 128), jnp.int32)
        ask = jnp.concatenate(rows + [near, lane, none], axis=0).T
        limit = jnp.concatenate(
            keys + [jnp.full((1, 128), TILES, jnp.int32), none], axis=0
        ).T
        found = jnp.full((128, 128), -1, jnp.int32)
        column_of = lax.broadcasted_iota(jnp.int32, (128, 128), 1)
        for r in range(4):
            best = jnp.full((128, 128), -1, jnp.int32)
            for c in range(3):
                match = (ask[:, r : r + 1] == given[c]) & (keys[c] < limit[:, r : r + 1])
                best = jnp.maximum(best, jnp.where(match, keys[c], -1))
            top = jnp.max(best, axis=1, keepdims=True)
            found = jnp.where(column_of == r, top, found)
        found = jnp.where(found < 0, TILES, found)
        rows_v[...] = found.T[0:8]

    def lists_end():
        local(rows_v, rows_s).wait()
        for copy in list_in:
            copy.wait_recv()
        local(lists_v, lists_s).wait()

    def half_forward_first(t, d):
        here = d % 4
        part_of = pl.ds(0 if d == 1 else 4, 4)
        ring = sets[t][0]
        mid_in[t, d].wait_recv()
        far_in[t, d] = remote(ring.at[here, part_of], ring.at[2, part_of], KINDS[t][0], d)

    def first_end(t):
        for d in (1, -1):
            copy = far_in.pop((t, d), None)
            if copy is not None:
                copy.wait_recv()

    def z_arrival(t, h):
        z_in[t, h].wait_recv()
        d = 1 if h > 0 else -1
        limit = reach[t][0] if h > 0 else reach[t][1]
        here = sets[t][0].at[h % 8]
        if abs(h) < limit:
            z_in[t, h + d] = remote(here, sets[t][0].at[(h + d) % 8], Z, d)
        for e in (1, -1):
            mid_in[t, e, h] = remote(here, sets[t][e % 4].at[h % 8], KINDS[t][1], e)

    def half_forward(t, e, h):
        q = h % 8
        half = pl.ds(0 if e == 1 else 4, 4)
        mid_in[t, e, h].wait_recv()
        far_in[t, e, h] = remote(
            sets[t][e % 4].at[q, half], sets[t][2].at[q, half], KINDS[t][1], e
        )

    def half_end(t):
        for h in (0, 1, -1, 2, -2, 3, -3, (-4, 4)[t]):
            for e in (1, -1):
                far_in[t, e, h].wait_recv()

    def wide_start(t, q):
        if q == 2:
            first_end(t)
        source = own(t) if q == 0 else sets[t][0].at[q]
        for d in (1, -1):
            wide_in[t, d, q] = remote(source, sets[t][d % 8].at[q], Z, d)

    def wide_arrival(t, h, q):
        wide_in[t, h, q].wait_recv()
        d = 1 if h > 0 else -1
        limit = reach[t][0] if h > 0 else reach[t][1]
        if abs(h) < limit:
            wide_in[t, h + d, q] = remote(
                sets[t][h % 8].at[q], sets[t][(h + d) % 8].at[q], Z, d
            )

    def pack(t, g):
        a, b, c = KINDS[t]
        if t > 1 and g == 0:
            first_end(t)
        if t < 2 and g == 2:
            half_end(t)
        n = SIZES[a]
        source = sets[t][g]
        target = packs[t]
        fixed = lax.rem(me[b] - g + SIZES[b], SIZES[b])
        rows = pl.ds(SLICE * t, SLICE)

        def spot(there, *rest):
            where = [None, None, None]
            where[c] = me[c]
            where[b] = fixed
            where[a] = there
            return (where[0], where[1], where[2]) + rest

        def one(j, carry):
            there = lax.rem(me[a] - j + n, n)
            owner = me[c] * STRIDES[c] + fixed * STRIDES[b] + there * STRIDES[a]
            for k in range(4):
                slot = 0 if k == 0 else (k if c == X else 3 + k)
                for s in range(2):
                    index = jnp.clip(lists_s[slot, s, owner], 0, NB - 1)
                    value = source[j, index]
                    if k == 0:
                        pulled[spot(there, s, rows, slice(None))] = value
                    else:
                        target[k - 1, g, there, s] = value
            return carry

        lax.fori_loop(0, n, one, 0)
        to = pulled.at[spot(slice(None), slice(None), rows, slice(None))]
        last_in[t, g] = [remote(target.at[k - 1, g], to, c, k) for k in (1, 3, 2)]

    def arrived(t, g):
        for copy in last_in[t, g]:
            copy.wait_recv()

    def local_tiles(start, stop):
        if start == 0:
            load_lt.wait()

        def eight(i, carry):
            values = []
            for j in range(8):
                k = i * 8 + j
                values.append(
                    jnp.dot(
                        lt[k], hist[lsrc_s[0, k]], preferred_element_type=jnp.float32
                    )
                )
            for j in range(8):
                k = i * 8 + j
                sums[k] = sums[rows_s[2, k]] + values[j]
            return carry

        lax.fori_loop(start, stop, eight, 0)

    def remote_tiles(n):
        g = order[n]
        first = LOCAL + 32 * n
        tiles = rt.at[n % SLOTS]
        z = lax.rem(me[2] - g + 8, 8)

        def eight(i, carry):
            values = []
            for j in range(4):
                for c in range(2):
                    values.append(
                        jnp.dot(
                            tiles[i, j, c], pulled[i, j, z, c], preferred_element_type=jnp.float32
                        )
                    )
            for j in range(4):
                o = i * 32 + j * 8 + z
                for c in range(2):
                    sums[first + i * 8 + j * 2 + c] = (
                        sums[rows_s[c, o]] + values[2 * j + c]
                    )
            return carry

        lax.fori_loop(0, 4, eight, 0)


    z_start(0)
    z_start(1)
    first_start(2)
    first_start(3)
    mid_start(0)
    mid_start(1)
    lists_start()
    for t in range(4):
        sets[t][0][0] = hist[:, SLICE * t : SLICE * (t + 1), :]
    index_rows()
    steps = {
        "z": z_arrival,
        "m": half_forward,
        "f": half_forward_first,
        "s": wide_start,
        "w": wide_arrival,
        "p": pack,
    }
    packed = 0
    for event in EVENTS:
        if event[0] == "p":
            if packed == 0:
                lists_end()
            packed += 1
        steps[event[0]](*event[1:])
        if event[0] == "p" and packed > 10 and packed <= 18:
            local_tiles(packed - 11, packed - 10)
    for t in (0, 1):
        for g in (0, 1, 3, 2):
            arrived(t, g)
    for n, g in enumerate(order):
        arrived(2, g)
        arrived(3, g)
        tiles_in[n].wait()
        remote_tiles(n)
        if n + SLOTS < 8:
            tiles_in.append(load_tiles(n + SLOTS))
    load_cot.wait()
    load_weight.wait()
    load_bias.wait()
    shifts = []
    for t in range(NB):
        following[t] = sums[rows_s[3, NB + t]].astype(jnp.bfloat16)
        shifts.append(send(following.at[t], coming.at[t], up, f))
    swaps = []
    w_mine = weight[pl.ds(pl.multiple_of(f * HALF, HALF), HALF), :]
    w_other = weight[pl.ds(pl.multiple_of((1 - f) * HALF, HALF), HALF), :]
    b = bias[...]
    g_mine = jnp.zeros((HALF, HALF), jnp.float32)
    g_other = jnp.zeros((HALF, HALF), jnp.float32)
    g_bias = jnp.zeros((8, HALF), jnp.float32)
    for u in range(NB + LAG):
        if u < NB:
            mine = sums[rows_s[3, u]]
            shifts[u].wait_recv()
            agg[u] = (mine + coming[u].astype(jnp.float32)).astype(jnp.bfloat16)
            swaps.append(send(agg.at[u], other.at[u], p, 1 - f))
        t = u - LAG
        if t < 0:
            continue
        swaps[t].wait_recv()
        a0 = agg[t]
        a1 = other[t]
        v = (
            jnp.dot(a0, w_mine, preferred_element_type=jnp.float32)
            + jnp.dot(a1, w_other, preferred_element_type=jnp.float32)
            + b
        )
        v2 = v * v
        th = jnp.tanh(ROOT * (v + CUBIC * (v2 * v)))
        half = 0.5 * (1.0 + th)
        rows = slice(BLK * t, BLK * (t + 1))
        new_rows[rows, :] = (v * half).astype(jnp.bfloat16)
        slope = half + (0.5 * ROOT) * v * (1.0 - th * th) * (1.0 + (3.0 * CUBIC) * v2)
        gp = (cot[rows, :].astype(jnp.float32) * slope).astype(jnp.bfloat16)
        dims = (((0,), (0,)), ((), ()))
        g_mine += lax.dot_general(a0, gp, dims, preferred_element_type=jnp.float32)
        g_other += lax.dot_general(a1, gp, dims, preferred_element_type=jnp.float32)
        g_bias += jnp.sum(gp.astype(jnp.float32).reshape(16, 8, HALF), axis=0)
    terms[pl.ds(f * 8, 8), 0:16, :] = g_mine.reshape(8, 16, HALF)
    terms[pl.ds((1 - f) * 8, 8), 0:16, :] = g_other.reshape(8, 16, HALF)
    terms[:, 16:24, :] = jnp.zeros((16, 8, HALF), jnp.float32)
    terms[0, 16:24, :] = g_bias

    spot = me[0] * 4 + me[1]
    ins = [send(terms.at[d // 8], part.at[i], d, f) for i, d in enumerate(flat)]
    total = terms[spot]
    for i in reversed(range(15)):
        ins[i].wait_recv()
        total = total + part[i]
    column_sums[me[2]] = total
    ins = [send(column_sums.at[me[2]], column_sums.at[me[2]], d, f) for d in column]
    for copy in ins:
        copy.wait_recv()
    total = column_sums[0]
    for k in range(1, 8):
        total = total + column_sums[k]
    final[spot] = total
    ins = [send(final.at[spot], final.at[spot], d, f) for d in flat]
    for copy in ins:
        copy.wait_recv()
    for k in range(16):
        grad_weight[16 * k : 16 * (k + 1), :] = final[k, 0:16, :]
    grad_bias[...] = jnp.sum(final[0, 16:24, :], axis=0, keepdims=True)
    for copy in remote_copies:
        copy.wait_send()


def step(*arrays):
    vm = pl.BlockSpec(memory_space=pltpu.VMEM)
    hbm = pl.BlockSpec(memory_space=pltpu.HBM)
    bf16 = jnp.bfloat16
    f32 = jnp.float32
    return pl.pallas_call(
        step_kernel,
        out_shape=(
            jax.ShapeDtypeStruct((NB * BLK, HALF), bf16),
            jax.ShapeDtypeStruct((2 * HALF, HALF), f32),
            jax.ShapeDtypeStruct((1, HALF), f32),
        ),
        in_specs=[hbm] * 10,
        out_specs=(vm, vm, vm),
        scratch_shapes=[pltpu.VMEM((8, NB, SLICE, HALF), bf16)] * 8
        + [pltpu.VMEM((4, NB, SLICE, HALF), bf16)] * 16
        + [pltpu.VMEM((3, 4, 8, 2, SLICE, HALF), bf16)] * 2
        + [pltpu.VMEM((3, 8, 4, 2, SLICE, HALF), bf16)] * 2
        + [
            pltpu.VMEM((7, 2, 128), jnp.int32),
            pltpu.SMEM((7, 2, 128), jnp.int32),
            pltpu.VMEM((2, 128), jnp.int32),
            pltpu.VMEM((1, 64), jnp.int32),
            pltpu.SMEM((1, 64), jnp.int32),
            pltpu.VMEM((8, 128), jnp.int32),
            pltpu.SMEM((8, 128), jnp.int32),
            pltpu.VMEM((2 * HALF, HALF), bf16),
            pltpu.VMEM((1, HALF), f32),
            pltpu.VMEM((NB, BLK, HALF), bf16),
            pltpu.VMEM((SLOTS, 4, 4, 2, BLK, BLK), bf16),
            pltpu.VMEM((LOCAL, BLK, BLK), bf16),
            pltpu.VMEM((NB * BLK, HALF), bf16),
            pltpu.VMEM((4, 4, 8, 2, BLK, HALF), bf16),
            pltpu.VMEM((TILES + 1, BLK, HALF), f32),
            pltpu.VMEM((NB, BLK, HALF), bf16),
            pltpu.VMEM((NB, BLK, HALF), bf16),
            pltpu.VMEM((NB, BLK, HALF), bf16),
            pltpu.VMEM((NB, BLK, HALF), bf16),
            pltpu.VMEM((16, PIECE, HALF), f32),
            pltpu.VMEM((15, PIECE, HALF), f32),
            pltpu.VMEM((8, PIECE, HALF), f32),
            pltpu.VMEM((16, PIECE, HALF), f32),
            pltpu.SemaphoreType.DMA((320,)),
            pltpu.SemaphoreType.DMA((320,)),
            pltpu.SemaphoreType.DMA((24,)),
        ],
        compiler_params=pltpu.CompilerParams(
            collective_id=0, has_side_effects=True, vmem_limit_bytes=51 << 20
        ),
        name="step",
    )(*[pltpu.with_memory_space_constraint(a, pltpu.HBM) for a in arrays])


def place_kernel(*refs):
    sems = refs[6]
    copies = [
        pltpu.make_async_copy(refs[i], refs[3 + i], sems.at[i]) for i in range(3)
    ]
    for copy in copies:
        copy.start()
    for copy in copies:
        copy.wait()


def place(*arrays):
    anywhere = pl.BlockSpec(memory_space=pl.ANY)
    return pl.pallas_call(
        place_kernel,
        out_shape=tuple(jax.ShapeDtypeStruct(a.shape, a.dtype) for a in arrays),
        in_specs=[anywhere] * 3,
        out_specs=(anywhere,) * 3,
        scratch_shapes=[pltpu.SemaphoreType.DMA((3,))],
        compiler_params=pltpu.CompilerParams(vmem_limit_bytes=4 << 20),
        name="place",
    )(*arrays)


def per_device(
    history,
    pull_list,
    remote_tiles,
    remote_dst,
    local_tiles,
    local_src,
    local_dst,
    weight,
    bias,
    cotangent,
):
    new_rows, grad_weight, grad_bias = step(
        history.reshape(NB, BLK, HALF),
        pull_list[0].T,
        remote_dst[0].T,
        local_src,
        local_dst,
        remote_tiles[0].reshape(4, 4, 8, 2, BLK, BLK),
        local_tiles,
        cotangent,
        weight,
        bias.reshape(1, HALF),
    )
    new_rows, grad_weight, grad_bias = place(new_rows, grad_weight, grad_bias)
    return new_rows, grad_weight, grad_bias.reshape(HALF)


def solution(mesh):
    placed = (
        P("dom", "feat"),
        P("dom", None, None),
        P("dom", None, None, None, None),
        P("dom", None, None),
        P("dom", None, None),
        P("dom", None),
        P("dom", None),
        P(None, "feat"),
        P("feat"),
        P("dom", "feat"),
    )
    return jax.shard_map(
        per_device,
        mesh=mesh,
        in_specs=placed,
        out_specs=(P("dom", "feat"), P(None, "feat"), P("feat")),
        check_vma=False,
    )
```

```python
import functools

import jax
import jax.numpy as jnp
from jax import lax
from jax.sharding import PartitionSpec as P
from jax.experimental import pallas as pl
from jax.experimental.pallas import tpu as pltpu

MESH = pl.DeviceIdType.MESH
X, Y, Z = 0, 1, 2
SIZES = (4, 4, 8)
STRIDES = (32, 8, 1)
NB = 8
BLK = 128
HALF = 128
SLICE = 32
KINDS = ((Z, Y, X), (Z, X, Y), (Y, Z, X), (X, Z, Y))


def coords():
    p = lax.axis_index("dom")
    return (p // 32, lax.rem(p // 8, 4), lax.rem(p, 8)), lax.axis_index("feat")


def group_rank(h):
    return jnp.where(h == 0, 0, jnp.where(h <= 4, 2 * h - 1, 2 * (8 - h)))


def moved(me, axis, offset):
    n = SIZES[axis]
    there = list(me)
    there[axis] = lax.rem(me[axis] + (offset % n), n)
    return there[0] * 32 + there[1] * 8 + there[2]


PIECE = 24
ROWS = pl.ds(0, 17)
ROOT = 0.7978845608028654
CUBIC = 0.044715
TILES = 320
LOCAL = 64
LAG = 2
SLOTS = 3
EVENTS = (
    ("s", 2, 0), ("z", 0, 1), ("z", 0, -1), ("f", 2, 1), ("f", 2, -1), ("f", 3, 1), ("f", 3, -1),
    ("z", 1, 1), ("z", 1, -1), ("m", 0, 1, 0), ("m", 0, -1, 0), ("m", 1, 1, 0), ("m", 1, -1, 0),
    ("w", 2, 1, 0), ("w", 2, -1, 0), ("m", 0, 1, 1), ("m", 0, -1, 1), ("m", 1, 1, 1), ("m", 1, -1, 1),
    ("p", 3, 0), ("z", 0, 2), ("z", 0, -2), ("m", 0, 1, -1), ("m", 0, -1, -1), ("p", 2, 0), ("m", 1, 1, -1),
    ("m", 1, -1, -1), ("z", 1, 2), ("z", 1, -2), ("w", 2, 2, 0), ("w", 2, -2, 0), ("z", 0, 3), ("z", 0, -3),
    ("s", 3, 0), ("z", 1, 3), ("z", 1, -3), ("m", 0, 1, 2), ("m", 0, -1, 2), ("w", 2, 3, 0), ("w", 2, -3, 0),
    ("s", 2, 1), ("m", 1, 1, 2), ("m", 1, -1, 2), ("m", 0, 1, -2), ("m", 0, -1, -2), ("w", 3, 1, 0),
    ("z", 0, -4), ("s", 2, 3), ("m", 1, 1, -2), ("m", 1, -1, -2), ("z", 1, 4), ("w", 3, -1, 0),
    ("m", 0, 1, 3), ("m", 0, -1, 3), ("m", 1, 1, 3), ("m", 1, -1, 3), ("w", 2, 4, 0), ("w", 2, -1, 1),
    ("m", 0, 1, -3), ("m", 0, -1, -3), ("m", 1, 1, -3), ("m", 1, -1, -3), ("w", 2, 1, 1), ("w", 2, -1, 3),
    ("p", 1, 0), ("p", 0, 0), ("w", 3, 2, 0), ("w", 3, -2, 0), ("m", 0, 1, -4), ("m", 0, -1, -4),
    ("m", 1, 1, 4), ("m", 1, -1, 4), ("w", 2, 1, 3), ("w", 2, -2, 1), ("w", 2, 2, 1), ("w", 2, -2, 3),
    ("w", 3, 3, 0), ("w", 3, -3, 0), ("s", 3, 1), ("p", 1, 1), ("w", 2, 2, 3), ("w", 2, -3, 1), ("p", 0, 1),
    ("w", 2, 3, 1), ("w", 2, -3, 3), ("s", 3, 3), ("w", 3, 1, 1), ("w", 3, -4, 0), ("s", 3, 2),
    ("w", 2, 3, 3), ("w", 3, -1, 1), ("p", 1, 3), ("p", 0, 3), ("s", 2, 2), ("w", 2, 4, 1), ("w", 3, -1, 3),
    ("w", 3, 1, 3), ("w", 3, -1, 2), ("w", 3, 2, 1), ("w", 3, -2, 1), ("w", 3, 1, 2), ("w", 2, -1, 2),
    ("p", 1, 2), ("p", 0, 2), ("w", 2, 4, 3), ("w", 3, -2, 3), ("w", 2, 1, 2), ("w", 3, -2, 2),
    ("w", 3, 2, 3), ("w", 3, -3, 1), ("w", 3, 3, 1), ("w", 2, -2, 2), ("p", 3, 7), ("w", 3, 2, 2),
    ("w", 3, -3, 3), ("p", 2, 7), ("w", 2, 2, 2), ("w", 3, -3, 2), ("p", 3, 1), ("w", 3, 3, 3),
    ("w", 3, -4, 1), ("p", 2, 1), ("w", 3, 3, 2), ("w", 2, -3, 2), ("p", 3, 6), ("w", 2, 3, 2),
    ("w", 3, -4, 3), ("p", 2, 6), ("w", 3, -4, 2), ("p", 3, 2), ("w", 2, 4, 2), ("p", 2, 2), ("p", 3, 5),
    ("p", 2, 5), ("p", 3, 3), ("p", 2, 3), ("p", 3, 4), ("p", 2, 4),
)


def step_kernel(
    history,
    plist,
    rdst,
    lsrc,
    ldst,
    rtiles,
    ltiles,
    cotangent,
    weight_hbm,
    bias_hbm,
    new_rows,
    grad_weight,
    grad_bias,
    *scratch,
):
    sets = [scratch[0:4], scratch[4:8], scratch[8:16], scratch[16:24]]
    packs = scratch[24:28]
    (
        lists_v,
        lists_s,
        rdst_v,
        ldst_v,
        lsrc_s,
        rows_v,
        rows_s,
        weight,
        bias,
        hist,
        rt,
        lt,
        cot,
        pulled,
        sums,
        following,
        coming,
        agg,
        other,
        terms,
        part,
        column_sums,
        final,
        send_sems,
        recv_sems,
        local_sems,
    ) = scratch[28:]
    me, f = coords()
    p = lax.axis_index("dom")
    used = [0, 0]
    remote_copies = []

    def send(src, dst, dom, feat):
        i = used[0]
        used[0] += 1
        copy = pltpu.make_async_remote_copy(
            src_ref=src,
            dst_ref=dst,
            send_sem=send_sems.at[i],
            recv_sem=recv_sems.at[i],
            device_id=(dom, feat),
            device_id_type=MESH,
        )
        copy.start()
        remote_copies.append(copy)
        return copy

    def remote(src, dst, axis, offset):
        return send(src, dst, moved(me, axis, offset), f)

    def local(src, dst):
        i = used[1]
        used[1] += 1
        copy = pltpu.make_async_copy(src, dst, local_sems.at[i])
        copy.start()
        return copy

    def own(t):
        return hist.at[:, pl.ds(SLICE * t, SLICE), :]

    load_hist = local(history, hist)
    small = [
        local(plist, lists_v.at[0]),
        local(rdst, rdst_v),
        local(ldst, ldst_v),
        local(lsrc, lsrc_s),
    ]
    up = lax.rem(p + 1, 128)
    column = [moved(me, Z, k) for k in (4, 3, 5, 2, 6, 1, 7)]
    flat = [
        lax.rem(me[0] + i, 4) * 32 + lax.rem(me[1] + j, 4) * 8 + me[2]
        for i, j in (
            ((2, 2), (2, 1), (1, 2), (2, 3), (3, 2), (1, 1), (1, 3), (3, 1), (3, 3))
            + ((2, 0), (0, 2), (1, 0), (0, 1), (3, 0), (0, 3))
        )
    ]
    barrier = pltpu.get_barrier_semaphore()
    near = ((X, 1), (X, 2), (X, 3), (Y, 1), (Y, 2), (Y, 3), (Z, 1), (Z, 7))
    greeted = [(p, 1 - f)] + [(moved(me, axis, k), f) for axis, k in near]
    for d in greeted:
        pl.semaphore_signal(barrier, inc=1, device_id=d, device_id_type=MESH)
    order = (0, 1, 7, 2, 6, 3, 5, 4)

    def load_tiles(i):
        z = lax.rem(me[2] - order[i] + 8, 8)
        return local(rtiles.at[:, :, z], rt.at[i % SLOTS])

    tiles_in = [load_tiles(i) for i in range(SLOTS)]
    load_lt = local(ltiles, lt)
    load_cot = local(cotangent, cot)
    load_weight = local(weight_hbm, weight)
    load_bias = local(bias_hbm, bias)
    sums[TILES] = jnp.zeros((BLK, HALF), jnp.float32)
    load_hist.wait()
    for copy in small:
        copy.wait()
    pl.semaphore_wait(barrier, len(greeted))

    z_in = {}
    mid_in = {}
    wide_in = {}
    far_in = {}
    last_in = {}
    list_in = []
    reach = {0: (3, 4), 1: (4, 3), 2: (4, 3), 3: (3, 4)}

    def z_start(t):
        for d in (1, -1):
            z_in[t, d] = remote(own(t), sets[t][0].at[d % 8], Z, d)

    def first_start(t):
        for d in (1, -1):
            mid_in[t, d] = remote(own(t), sets[t][0].at[d % 4], KINDS[t][0], d)

    def mid_start(t):
        for d in (1, -1):
            mid_in[t, d, 0] = remote(own(t), sets[t][d % 4].at[0], KINDS[t][1], d)

    def lists_start():
        for i, axis in enumerate((X, Y)):
            for k in (1, 2, 3):
                list_in.append(remote(lists_v.at[0], lists_v.at[3 * i + k], axis, -k))

    def index_rows():
        lane = lax.broadcasted_iota(jnp.int32, (1, 128), 1)
        h = lax.rem(me[2] - lax.rem(lane, 8) + 8, 8)
        key = LOCAL + group_rank(h) * 32 + (lane // 32) * 8 + lax.rem(lane // 8, 4) * 2
        wanted = lists_v[0]
        there = rdst_v[...]
        near = jnp.concatenate([ldst_v[...], jnp.full((1, 64), -1, jnp.int32)], axis=1)
        rows = [there[0:1], there[1:2]]
        given = [jnp.where(wanted[c : c + 1] >= 0, rows[c], -1) for c in range(2)] + [near]
        keys = [key, key + 1, lane]
        none = jnp.zeros((4, 128), jnp.int32)
        ask = jnp.concatenate(rows + [near, lane, none], axis=0).T
        limit = jnp.concatenate(
            keys + [jnp.full((1, 128), TILES, jnp.int32), none], axis=0
        ).T
        found = jnp.full((128, 128), -1, jnp.int32)
        column_of = lax.broadcasted_iota(jnp.int32, (128, 128), 1)
        for r in range(4):
            best = jnp.full((128, 128), -1, jnp.int32)
            for c in range(3):
                match = (ask[:, r : r + 1] == given[c]) & (keys[c] < limit[:, r : r + 1])
                best = jnp.maximum(best, jnp.where(match, keys[c], -1))
            top = jnp.max(best, axis=1, keepdims=True)
            found = jnp.where(column_of == r, top, found)
        found = jnp.where(found < 0, TILES, found)
        rows_v[...] = found.T[0:8]

    def lists_end():
        local(rows_v, rows_s).wait()
        for copy in list_in:
            copy.wait_recv()
        local(lists_v, lists_s).wait()

    def half_forward_first(t, d):
        here = d % 4
        part_of = pl.ds(0 if d == 1 else 4, 4)
        ring = sets[t][0]
        mid_in[t, d].wait_recv()
        far_in[t, d] = remote(ring.at[here, part_of], ring.at[2, part_of], KINDS[t][0], d)

    def first_end(t):
        for d in (1, -1):
            copy = far_in.pop((t, d), None)
            if copy is not None:
                copy.wait_recv()

    def z_arrival(t, h):
        z_in[t, h].wait_recv()
        d = 1 if h > 0 else -1
        limit = reach[t][0] if h > 0 else reach[t][1]
        here = sets[t][0].at[h % 8]
        if abs(h) < limit:
            z_in[t, h + d] = remote(here, sets[t][0].at[(h + d) % 8], Z, d)
        for e in (1, -1):
            mid_in[t, e, h] = remote(here, sets[t][e % 4].at[h % 8], KINDS[t][1], e)

    def half_forward(t, e, h):
        q = h % 8
        half = pl.ds(0 if e == 1 else 4, 4)
        mid_in[t, e, h].wait_recv()
        far_in[t, e, h] = remote(
            sets[t][e % 4].at[q, half], sets[t][2].at[q, half], KINDS[t][1], e
        )

    def half_end(t):
        for h in (0, 1, -1, 2, -2, 3, -3, (-4, 4)[t]):
            for e in (1, -1):
                far_in[t, e, h].wait_recv()

    def wide_start(t, q):
        if q == 2:
            first_end(t)
        source = own(t) if q == 0 else sets[t][0].at[q]
        for d in (1, -1):
            wide_in[t, d, q] = remote(source, sets[t][d % 8].at[q], Z, d)

    def wide_arrival(t, h, q):
        wide_in[t, h, q].wait_recv()
        d = 1 if h > 0 else -1
        limit = reach[t][0] if h > 0 else reach[t][1]
        if abs(h) < limit:
            wide_in[t, h + d, q] = remote(
                sets[t][h % 8].at[q], sets[t][(h + d) % 8].at[q], Z, d
            )

    def pack(t, g):
        a, b, c = KINDS[t]
        if t > 1 and g == 0:
            first_end(t)
        if t < 2 and g == 2:
            half_end(t)
        n = SIZES[a]
        source = sets[t][g]
        target = packs[t]
        fixed = lax.rem(me[b] - g + SIZES[b], SIZES[b])
        rows = pl.ds(SLICE * t, SLICE)

        def spot(there, *rest):
            where = [None, None, None]
            where[c] = me[c]
            where[b] = fixed
            where[a] = there
            return (where[0], where[1], where[2]) + rest

        def one(j, carry):
            there = lax.rem(me[a] - j + n, n)
            owner = me[c] * STRIDES[c] + fixed * STRIDES[b] + there * STRIDES[a]
            for k in range(4):
                slot = 0 if k == 0 else (k if c == X else 3 + k)
                for s in range(2):
                    index = jnp.clip(lists_s[slot, s, owner], 0, NB - 1)
                    value = source[j, index]
                    if k == 0:
                        pulled[spot(there, s, rows, slice(None))] = value
                    else:
                        target[k - 1, g, there, s] = value
            return carry

        lax.fori_loop(0, n, one, 0)
        to = pulled.at[spot(slice(None), slice(None), rows, slice(None))]
        last_in[t, g] = [remote(target.at[k - 1, g], to, c, k) for k in (1, 3, 2)]

    def arrived(t, g):
        for copy in last_in[t, g]:
            copy.wait_recv()

    def local_tiles(start, stop):
        if start == 0:
            load_lt.wait()

        def eight(i, carry):
            values = []
            for j in range(8):
                k = i * 8 + j
                values.append(
                    jnp.dot(
                        lt[k], hist[lsrc_s[0, k]], preferred_element_type=jnp.float32
                    )
                )
            for j in range(8):
                k = i * 8 + j
                sums[k] = sums[rows_s[2, k]] + values[j]
            return carry

        lax.fori_loop(start, stop, eight, 0)

    def remote_tiles(n):
        g = order[n]
        first = LOCAL + 32 * n
        tiles = rt.at[n % SLOTS]
        z = lax.rem(me[2] - g + 8, 8)

        def eight(i, carry):
            values = []
            for j in range(4):
                for c in range(2):
                    values.append(
                        jnp.dot(
                            tiles[i, j, c], pulled[i, j, z, c], preferred_element_type=jnp.float32
                        )
                    )
            for j in range(4):
                o = i * 32 + j * 8 + z
                for c in range(2):
                    sums[first + i * 8 + j * 2 + c] = (
                        sums[rows_s[c, o]] + values[2 * j + c]
                    )
            return carry

        for i in range(4):
            eight(i, 0)


    z_start(0)
    z_start(1)
    first_start(2)
    first_start(3)
    mid_start(0)
    mid_start(1)
    lists_start()
    for t in range(4):
        sets[t][0][0] = hist[:, SLICE * t : SLICE * (t + 1), :]
    index_rows()
    steps = {
        "z": z_arrival,
        "m": half_forward,
        "f": half_forward_first,
        "s": wide_start,
        "w": wide_arrival,
        "p": pack,
    }
    packed = 0
    for event in EVENTS:
        if event[0] == "p":
            if packed == 0:
                lists_end()
            packed += 1
        steps[event[0]](*event[1:])
        if event[0] == "p" and packed > 10 and packed <= 18:
            local_tiles(packed - 11, packed - 10)
    for t in (0, 1):
        for g in (0, 1, 3, 2):
            arrived(t, g)
    for n, g in enumerate(order):
        arrived(2, g)
        arrived(3, g)
        tiles_in[n].wait()
        remote_tiles(n)
        if n + SLOTS < 8:
            tiles_in.append(load_tiles(n + SLOTS))
    load_cot.wait()
    load_weight.wait()
    load_bias.wait()
    shifts = []
    for t in range(NB):
        following[t] = sums[rows_s[3, NB + t]].astype(jnp.bfloat16)
        shifts.append(send(following.at[t], coming.at[t], up, f))
    swaps = []
    w_mine = weight[pl.ds(pl.multiple_of(f * HALF, HALF), HALF), :]
    w_other = weight[pl.ds(pl.multiple_of((1 - f) * HALF, HALF), HALF), :]
    b = bias[...]
    g_mine = jnp.zeros((HALF, HALF), jnp.float32)
    g_other = jnp.zeros((HALF, HALF), jnp.float32)
    g_bias = jnp.zeros((8, HALF), jnp.float32)
    for u in range(NB + LAG):
        if u < NB:
            mine = sums[rows_s[3, u]]
            shifts[u].wait_recv()
            agg[u] = (mine + coming[u].astype(jnp.float32)).astype(jnp.bfloat16)
            swaps.append(send(agg.at[u], other.at[u], p, 1 - f))
        t = u - LAG
        if t < 0:
            continue
        swaps[t].wait_recv()
        a0 = agg[t]
        a1 = other[t]
        v = (
            jnp.dot(a0, w_mine, preferred_element_type=jnp.float32)
            + jnp.dot(a1, w_other, preferred_element_type=jnp.float32)
            + b
        )
        v2 = v * v
        th = jnp.tanh(ROOT * (v + CUBIC * (v2 * v)))
        half = 0.5 * (1.0 + th)
        rows = slice(BLK * t, BLK * (t + 1))
        new_rows[rows, :] = (v * half).astype(jnp.bfloat16)
        slope = half + (0.5 * ROOT) * v * (1.0 - th * th) * (1.0 + (3.0 * CUBIC) * v2)
        gp = (cot[rows, :].astype(jnp.float32) * slope).astype(jnp.bfloat16)
        dims = (((0,), (0,)), ((), ()))
        g_mine += lax.dot_general(a0, gp, dims, preferred_element_type=jnp.float32)
        g_other += lax.dot_general(a1, gp, dims, preferred_element_type=jnp.float32)
        g_bias += jnp.sum(gp.astype(jnp.float32).reshape(16, 8, HALF), axis=0)
    terms[pl.ds(f * 8, 8), 0:16, :] = g_mine.reshape(8, 16, HALF)
    terms[pl.ds((1 - f) * 8, 8), 0:16, :] = g_other.reshape(8, 16, HALF)
    terms[:, 16:24, :] = jnp.zeros((16, 8, HALF), jnp.float32)
    terms[0, 16:17, :] = jnp.sum(g_bias, axis=0, keepdims=True)

    spot = me[0] * 4 + me[1]
    ins = [send(terms.at[d // 8, ROWS], part.at[i, ROWS], d, f) for i, d in enumerate(flat)]
    total = terms[spot, 0:17]
    for i in reversed(range(15)):
        ins[i].wait_recv()
        total = total + part[i, 0:17]
    column_sums[me[2], 0:17] = total
    ins = [send(column_sums.at[me[2], ROWS], column_sums.at[me[2], ROWS], d, f) for d in column]
    for copy in ins:
        copy.wait_recv()
    total = column_sums[0, 0:17]
    for k in range(1, 8):
        total = total + column_sums[k, 0:17]
    final[spot, 0:17] = total
    ins = [send(final.at[spot, ROWS], final.at[spot, ROWS], d, f) for d in flat]
    for copy in ins:
        copy.wait_recv()
    for k in range(16):
        grad_weight[16 * k : 16 * (k + 1), :] = final[k, 0:16, :]
    grad_bias[...] = final[0, 16:17, :]
    for copy in remote_copies:
        copy.wait_send()


def step(*arrays):
    vm = pl.BlockSpec(memory_space=pltpu.VMEM)
    hbm = pl.BlockSpec(memory_space=pltpu.HBM)
    bf16 = jnp.bfloat16
    f32 = jnp.float32
    return pl.pallas_call(
        step_kernel,
        out_shape=(
            jax.ShapeDtypeStruct((NB * BLK, HALF), bf16),
            jax.ShapeDtypeStruct((2 * HALF, HALF), f32),
            jax.ShapeDtypeStruct((1, HALF), f32),
        ),
        in_specs=[hbm] * 10,
        out_specs=(vm, vm, vm),
        scratch_shapes=[pltpu.VMEM((8, NB, SLICE, HALF), bf16)] * 8
        + [pltpu.VMEM((4, NB, SLICE, HALF), bf16)] * 16
        + [pltpu.VMEM((3, 4, 8, 2, SLICE, HALF), bf16)] * 2
        + [pltpu.VMEM((3, 8, 4, 2, SLICE, HALF), bf16)] * 2
        + [
            pltpu.VMEM((7, 2, 128), jnp.int32),
            pltpu.SMEM((7, 2, 128), jnp.int32),
            pltpu.VMEM((2, 128), jnp.int32),
            pltpu.VMEM((1, 64), jnp.int32),
            pltpu.SMEM((1, 64), jnp.int32),
            pltpu.VMEM((8, 128), jnp.int32),
            pltpu.SMEM((8, 128), jnp.int32),
            pltpu.VMEM((2 * HALF, HALF), bf16),
            pltpu.VMEM((1, HALF), f32),
            pltpu.VMEM((NB, BLK, HALF), bf16),
            pltpu.VMEM((SLOTS, 4, 4, 2, BLK, BLK), bf16),
            pltpu.VMEM((LOCAL, BLK, BLK), bf16),
            pltpu.VMEM((NB * BLK, HALF), bf16),
            pltpu.VMEM((4, 4, 8, 2, BLK, HALF), bf16),
            pltpu.VMEM((TILES + 1, BLK, HALF), f32),
            pltpu.VMEM((NB, BLK, HALF), bf16),
            pltpu.VMEM((NB, BLK, HALF), bf16),
            pltpu.VMEM((NB, BLK, HALF), bf16),
            pltpu.VMEM((NB, BLK, HALF), bf16),
            pltpu.VMEM((16, PIECE, HALF), f32),
            pltpu.VMEM((15, PIECE, HALF), f32),
            pltpu.VMEM((8, PIECE, HALF), f32),
            pltpu.VMEM((16, PIECE, HALF), f32),
            pltpu.SemaphoreType.DMA((320,)),
            pltpu.SemaphoreType.DMA((320,)),
            pltpu.SemaphoreType.DMA((24,)),
        ],
        compiler_params=pltpu.CompilerParams(
            collective_id=0, has_side_effects=True, vmem_limit_bytes=51 << 20
        ),
        name="step",
    )(*[pltpu.with_memory_space_constraint(a, pltpu.HBM) for a in arrays])


def place_kernel(*refs):
    sems = refs[6]
    copies = [
        pltpu.make_async_copy(refs[i], refs[3 + i], sems.at[i]) for i in range(3)
    ]
    for copy in copies:
        copy.start()
    for copy in copies:
        copy.wait()


def place(*arrays):
    anywhere = pl.BlockSpec(memory_space=pl.ANY)
    return pl.pallas_call(
        place_kernel,
        out_shape=tuple(jax.ShapeDtypeStruct(a.shape, a.dtype) for a in arrays),
        in_specs=[anywhere] * 3,
        out_specs=(anywhere,) * 3,
        scratch_shapes=[pltpu.SemaphoreType.DMA((3,))],
        compiler_params=pltpu.CompilerParams(vmem_limit_bytes=4 << 20),
        name="place",
    )(*arrays)


def per_device(
    history,
    pull_list,
    remote_tiles,
    remote_dst,
    local_tiles,
    local_src,
    local_dst,
    weight,
    bias,
    cotangent,
):
    new_rows, grad_weight, grad_bias = step(
        history.reshape(NB, BLK, HALF),
        pull_list[0].T,
        remote_dst[0].T,
        local_src,
        local_dst,
        remote_tiles[0].reshape(4, 4, 8, 2, BLK, BLK),
        local_tiles,
        cotangent,
        weight,
        bias.reshape(1, HALF),
    )
    new_rows, grad_weight, grad_bias = place(new_rows, grad_weight, grad_bias)
    return new_rows, grad_weight, grad_bias.reshape(HALF)


def solution(mesh):
    placed = (
        P("dom", "feat"),
        P("dom", None, None),
        P("dom", None, None, None, None),
        P("dom", None, None),
        P("dom", None, None),
        P("dom", None),
        P("dom", None),
        P(None, "feat"),
        P("feat"),
        P("dom", "feat"),
    )
    return jax.shard_map(
        per_device,
        mesh=mesh,
        in_specs=placed,
        out_specs=(P("dom", "feat"), P(None, "feat"), P("feat")),
        check_vma=False,
    )
```
